512 devices in a mesh: region: 256 (over z, y, x), dom: 2 (over core).
Axes of the slice: x: 4, y: 8, z: 8, core: 2. Of those that a mesh axis runs over, the one named last changes fastest.
Arguments:
- fine_state: float32 [262144, 128], P(('region', 'dom')), may hold values from -6 to 6
- fine_nbr: int32 [16, 262144], P(None, ('region', 'dom')), may hold values from 0 to 575
- fine_mask: int32 [16, 262144], P(None, ('region', 'dom')), may hold values 0 or 1
- send_rows: int32 [4, 8192], P(None, ('region', 'dom')), may hold values from 0 to 511
- coarse_nbr: int32 [16, 65536], P(None, ('region', 'dom')), may hold values from 0 to 255
- coarse_mask: int32 [16, 65536], P(None, ('region', 'dom')), may hold values 0 or 1
- parent: int32 [262144], P(('region', 'dom')), may hold values from 0 to 65535, as said below
- interp_share: int32 [262144], P(('region', 'dom')), may hold values from 1 to 4
- edge_w: float32 [4, 3, 128, 128], replicated, may hold values from -0.375 to 0.375
- node_w: float32 [4, 3, 128, 128], replicated, may hold values from -0.375 to 0.375
- biases: float32 [4, 4, 128], replicated, may hold values from -3 to 3
Outputs:
- fine_out: float32 [262144, 128], P(('region', 'dom'))
- coarse_out: float32 [65536, 128], P(('region', 'dom'))
The draws below stay inside these ranges and needn't reach their ends.
Inputs may be any that keep to these rules, and one draw needn't show every extreme that they name: `parent`: of the 512 fine nodes of block (r, d), 448 have parents in coarse blocks of region r, at most 384 in any one block and exactly 384 in some block; 32 have parents in blocks of region r-1 and 32 in blocks of region r+1 (periodic), at most 32 in any one block and exactly 32 in some block of each.
All inputs are finite; a program needn't handle non-finite values. No bound on the sum of `fine_mask` or of `coarse_mask` on one device may be relied on, other than what follows from the above.
Results may differ from the reference program's by a relative error of at most 0.0001.
Values sent between devices are 32-bit elements; how exact they have to be, the bound alone decides.
A program may use at most 64 MiB of HBM per device.

```python
import jax
import jax.numpy as jnp
from jax import lax

W = 128
SLOTS = 16
LAYERS = 4
F = 512
H = 16
C = 128
SIDE = 32
CAP = 384
SCAP = 32
FN = 262144
CN = 65536
RC = 256
N_REGION = 256
N_DOM = 2
DEVICES = 512


def bin_counts(count_key, bins, total, most):
    split_keys = jax.random.split(count_key, 2)
    big_bin = jax.random.randint(split_keys[0], (), 0, bins)
    units = (bins - 1) * most
    unit_label = jnp.arange(units, dtype=jnp.int32) // most
    shuffled = jax.random.permutation(split_keys[1], units)
    taken = (jnp.arange(units, dtype=jnp.int32) < total - most).astype(jnp.int32)
    extra = jnp.zeros((bins - 1,), jnp.int32).at[unit_label[shuffled]].add(taken)
    positions = jnp.arange(bins, dtype=jnp.int32)
    other_index = jnp.clip(positions - (positions > big_bin).astype(jnp.int32), 0, bins - 2)
    return jnp.where(positions == big_bin, most, extra[other_index]).astype(jnp.int32)


def labels_of(counts, length):
    ends = jnp.cumsum(counts)
    return jnp.sum((ends[None, :] <= jnp.arange(length, dtype=jnp.int32)[:, None]).astype(jnp.int32), axis=1)


def owner_draw(device_key, device_number):
    split_keys = jax.random.split(device_key, 5)
    own_len = F - 2 * SIDE
    region_now = device_number // N_DOM
    own_dom = labels_of(bin_counts(split_keys[0], N_DOM, own_len, CAP), own_len)
    low_dom = labels_of(bin_counts(split_keys[1], N_DOM, SIDE, SCAP), SIDE)
    high_dom = labels_of(bin_counts(split_keys[2], N_DOM, SIDE, SCAP), SIDE)
    regions_of = jnp.concatenate([jnp.zeros((own_len,), jnp.int32) + region_now, jnp.zeros((SIDE,), jnp.int32) + (region_now + N_REGION - 1) % N_REGION, jnp.zeros((SIDE,), jnp.int32) + (region_now + 1) % N_REGION])
    doms_of = jnp.concatenate([own_dom, low_dom, high_dom])
    owner_dev = regions_of * N_DOM + doms_of
    owner_dev = owner_dev[jax.random.permutation(split_keys[3], F)]
    local_parent = jax.random.randint(split_keys[4], (F,), 0, C)
    return (owner_dev * C + local_parent).astype(jnp.int32)


def draw_parent(key, part):
    device_keys = jax.random.split(key, DEVICES)
    numbers = jnp.arange(DEVICES, dtype=jnp.int32)
    return jax.vmap(owner_draw)(device_keys, numbers).reshape(FN).astype(jnp.int32)


def touch_ends(values, stream_key, low, high):
    shape = values.shape
    spot = [jax.random.randint(jax.random.fold_in(stream_key, axis), (), 0, shape[axis]) for axis in range(len(shape))]
    values = values.at[tuple(spot)].set(low)
    longest = shape.index(max(shape))
    spot[longest] = (spot[longest] + 1) % shape[longest]
    return values.at[tuple(spot)].set(high)


def steps_of(own_key, dims, cuts, smallest, top_value):
    def one(axis_at, parts):
        heights = jax.random.uniform(jax.random.fold_in(jax.random.fold_in(own_key, 6), axis_at), (parts,), jnp.float32, smallest / len(cuts), top_value / len(cuts))
        return jnp.repeat(jnp.exp(heights), dims[axis_at] // parts).reshape((-1,) + (1,) * (len(dims) - axis_at - 1))

    loudness = one(*cuts[0])
    for cut in cuts[1:]:
        loudness = loudness * one(*cut)
    return loudness


def scatter_about(stream_key, shape, scale, most, cuts=(), kind=jnp.bfloat16):
    result = jax.random.normal(stream_key, shape, jnp.float32) * scale
    if len(cuts) > 0:
        result = steps_of(stream_key, shape, cuts, -0.22, 0.18) * result
    return jnp.clip(result, min=-most, max=most).astype(kind)


def setup_inputs(seed: int = 0) -> dict:
    key_list = jax.random.split(jax.random.key(seed), 12)
    fine_state = scatter_about(key_list[0], (FN, W), 1.0, 6.0, ((0, 512),), jnp.float32)
    fine_nbr = touch_ends(jax.random.randint(key_list[1], (SLOTS, FN), 0, F + 4 * H), jax.random.fold_in(key_list[1], 1), 0, (F + 4 * H) - 1).astype(jnp.int32)
    fine_mask = touch_ends((jax.random.randint(key_list[2], (SLOTS, FN), 0, 16) < 13).astype(jnp.int32), jax.random.fold_in(key_list[2], 1), 0, 1)
    send_rows = touch_ends(jax.random.randint(key_list[3], (4, DEVICES * H), 0, F), jax.random.fold_in(key_list[3], 1), 0, F - 1).astype(jnp.int32)
    coarse_nbr = touch_ends(jax.random.randint(key_list[4], (SLOTS, CN), 0, RC), jax.random.fold_in(key_list[4], 1), 0, RC - 1).astype(jnp.int32)
    coarse_mask = touch_ends((jax.random.randint(key_list[5], (SLOTS, CN), 0, 16) < 13).astype(jnp.int32), jax.random.fold_in(key_list[5], 1), 0, 1)
    parent = draw_parent(jax.random.fold_in(key_list[11], 71), 0)
    interp_share = touch_ends(jax.random.randint(key_list[7], (FN,), 1, 5), jax.random.fold_in(key_list[7], 1), 1, 4).astype(jnp.int32)
    edge_w = scatter_about(key_list[8], (LAYERS, 3, W, W), (2 * W) ** -0.5, 0.375, (), jnp.float32)
    node_w = scatter_about(key_list[9], (LAYERS, 3, W, W), (2 * W) ** -0.5, 0.375, (), jnp.float32)
    biases = scatter_about(key_list[10], (LAYERS, 4, W), 0.5, 3.0, (), jnp.float32)
    return {"fine_state": fine_state, "fine_nbr": fine_nbr, "fine_mask": fine_mask, "send_rows": send_rows, "coarse_nbr": coarse_nbr, "coarse_mask": coarse_mask, "parent": parent, "interp_share": interp_share, "edge_w": edge_w, "node_w": node_w, "biases": biases}


epsilon = 1e-05

def product(left_side, right_side):
    return jnp.dot(left_side, right_side, precision=lax.Precision.HIGHEST, preferred_element_type=jnp.float32)

def normed(values):
    center = values - lax.optimization_barrier(jnp.mean(values, axis=-1, keepdims=True))
    spread = lax.optimization_barrier(jnp.mean(center * center, axis=-1, keepdims=True))
    return center * lax.rsqrt(spread + epsilon)

def message_layer(own_rows, source_proj, neighbours, validity, edge_w, node_w, biases, layer_idx):
    own_term = product(own_rows, edge_w[layer_idx, 0]) + biases[layer_idx, 0]

    def one_slot(running, slot_data):
        index_row, valid_row = slot_data
        hidden = jax.nn.relu(own_term + jnp.take(source_proj, index_row, axis=0))
        message = normed(product(hidden, edge_w[layer_idx, 2]) + biases[layer_idx, 1])
        return (running + valid_row.astype(jnp.float32)[:, None] * message, None)
    gathered, unused = lax.scan(one_slot, jnp.zeros(own_rows.shape, jnp.float32), (neighbours, validity))
    inner_act = jax.nn.relu(product(own_rows, node_w[layer_idx, 0]) + product(gathered, node_w[layer_idx, 1]) + biases[layer_idx, 2])
    return own_rows + normed(product(inner_act, node_w[layer_idx, 2]) + biases[layer_idx, 3])

def fine_layer(fine_rows, fine_nbr, fine_mask, send_rows, edge_w, node_w, biases, layer_idx):
    device_grid = fine_rows.reshape(N_REGION, N_DOM, F, W)
    send_lists = send_rows.reshape(4, N_REGION, N_DOM, H)

    def picked(direction):
        return jnp.take_along_axis(device_grid, send_lists[direction][..., None], axis=2)
    from_region_low = jnp.roll(picked(0), 1, axis=0)
    from_region_high = jnp.roll(picked(1), -1, axis=0)
    from_dom_low = jnp.roll(picked(2), 1, axis=1)
    from_dom_high = jnp.roll(picked(3), -1, axis=1)
    extended = jnp.concatenate([device_grid, from_region_low, from_region_high, from_dom_low, from_dom_high], axis=2)
    extended = extended.reshape(DEVICES, F + 4 * H, W)
    own_blocks = fine_rows.reshape(DEVICES, F, W)
    nbr_blocks = fine_nbr.reshape(SLOTS, DEVICES, F).transpose(1, 0, 2)
    mask_blocks = fine_mask.reshape(SLOTS, DEVICES, F).transpose(1, 0, 2)

    def per_device(device_items):
        own_rows, ext_rows, nbr_rows, mask_rows = device_items
        return message_layer(own_rows, product(ext_rows, edge_w[layer_idx, 1]), nbr_rows, mask_rows, edge_w, node_w, biases, layer_idx)
    return lax.map(per_device, (own_blocks, extended, nbr_blocks, mask_blocks)).reshape(FN, W)

def coarse_layer(coarse_rows, coarse_nbr, coarse_mask, edge_w, node_w, biases, layer_idx):
    grouped = coarse_rows.reshape(N_REGION, RC, W)
    nbr_groups = coarse_nbr.reshape(SLOTS, N_REGION, RC).transpose(1, 0, 2)
    mask_groups = coarse_mask.reshape(SLOTS, N_REGION, RC).transpose(1, 0, 2)

    def per_region(region_items):
        own_rows, nbr_rows, mask_rows = region_items
        return message_layer(own_rows, product(own_rows, edge_w[layer_idx, 1]), nbr_rows, mask_rows, edge_w, node_w, biases, layer_idx)
    return lax.map(per_region, (grouped, nbr_groups, mask_groups)).reshape(CN, W)

def reference(fine_state, fine_nbr, fine_mask, send_rows, coarse_nbr, coarse_mask, parent, interp_share, edge_w, node_w, biases):
    fine_rows = fine_layer(fine_state, fine_nbr, fine_mask, send_rows, edge_w, node_w, biases, 0)
    weights_num = interp_share.astype(jnp.float32)
    summed = jax.ops.segment_sum(weights_num[:, None] * fine_rows, parent, num_segments=CN)
    totals = jax.ops.segment_sum(weights_num, parent, num_segments=CN)
    coarse_rows = summed / jnp.maximum(totals, 1.0)[:, None]
    coarse_rows = coarse_layer(coarse_rows, coarse_nbr, coarse_mask, edge_w, node_w, biases, 1)
    coarse_rows = coarse_layer(coarse_rows, coarse_nbr, coarse_mask, edge_w, node_w, biases, 2)
    fine_rows = fine_rows + (weights_num / 4.0)[:, None] * jnp.take(coarse_rows, parent, axis=0)
    fine_rows = fine_layer(fine_rows, fine_nbr, fine_mask, send_rows, edge_w, node_w, biases, 3)
    return (fine_rows, coarse_rows)
```

```python
import functools

import jax
import jax.numpy as jnp
from jax import lax
from jax.experimental import pallas as pl
from jax.experimental.pallas import tpu as pltpu
from jax.sharding import PartitionSpec as P

MESH = pl.DeviceIdType.MESH
EPS = 1e-05
F32 = jnp.float32
BF16 = jnp.bfloat16
W = 128
SLOTS = 16
F = 512
H = 16
C = 128
SIDE = 32


def halves(x):
    hi = x.astype(BF16)
    lo = (x - hi.astype(F32)).astype(BF16)
    return hi, lo


def split(x):
    return jnp.concatenate(halves(x), axis=0)


def dot(a, b):
    return lax.dot_general(a, b, (((1,), (0,)), ((), ())), preferred_element_type=F32)


def dot_nt(a, b):
    return lax.dot_general(a, b, (((1,), (1,)), ((), ())), preferred_element_type=F32)


def fold(y):
    return y[:W] + y[W:]


def fold_lanes(y):
    return y[:, :W] + y[:, W:]


def one_hot(index_row, depth):
    n = index_row.shape[1]
    blocks = []
    for base in range(0, depth, 256):
        size = min(256, depth - base)
        rows = lax.broadcasted_iota(jnp.int32, (size, n), 0)
        blocks.append((rows == (index_row - base)).astype(F32).astype(BF16))
    return blocks[0] if len(blocks) == 1 else jnp.concatenate(blocks, axis=0)


def stacked(w, centred=False):
    t = w.T
    if centred:
        t = t - jnp.sum(t, axis=0, keepdims=True) * (1.0 / W)
    s = split(t)
    return jnp.concatenate([s, s], axis=1)


def scale_of(centred):
    return lax.rsqrt(jnp.sum(centred * centred, axis=0, keepdims=True) * (1.0 / W) + EPS)


def centred_bias(column):
    return column - jnp.sum(column, axis=0, keepdims=True) * (1.0 / W)


def message(gathered, own, second, second_bias, valid_row):
    hidden = jnp.maximum(fold(gathered) + own, 0.0)
    centred = fold(dot(second, split(hidden))) + second_bias
    return centred * (scale_of(centred) * valid_row)


def node_update(rows, own_part, total, node1, node2, bias3):
    inner = jnp.maximum(own_part + fold(dot(node1, split(total))), 0.0)
    centred = fold(dot(node2, split(inner))) + bias3
    return rows + centred * scale_of(centred)


def kernel(
    regions,
    x_ref,
    nbr_ref,
    mask_ref,
    send_ref,
    cnbr_ref,
    cmask_ref,
    parent_ref,
    share_ref,
    edge_ref,
    node_ref,
    bias_ref,
    out_ref,
    cout_ref,
    tile_ref,
    wts,
    src_proj,
    own_ref,
    node_own,
    total_ref,
    fine_ref,
    rim_pick,
    side_pick,
    own_hot,
    rim_send,
    rim_recv,
    meta_send,
    meta_recv,
    tot_send,
    tot_recv,
    part_send,
    part_recv,
    side_send,
    side_recv,
    mid_send,
    mid_recv,
    co_send,
    co_recv,
    reply_send,
    reply_recv,
    rim2_send,
    rim2_recv,
    send_sem,
    recv_sem,
):
    r = lax.axis_index("region")
    d = lax.axis_index("dom")
    up = lax.rem(r + 1, regions)
    down = lax.rem(r + regions - 1, regions)
    other = 1 - d
    peers = [(down, 0), (down, 1), (up, 0), (up, 1), (r, other)]
    barrier = pltpu.get_barrier_semaphore()
    for peer in peers:
        pl.semaphore_signal(barrier, inc=1, device_id=peer, device_id_type=MESH)

    def copy(k, src, dst, peer):
        return pltpu.make_async_remote_copy(
            src_ref=src,
            dst_ref=dst,
            send_sem=send_sem.at[k],
            recv_sem=recv_sem.at[k],
            device_id=peer,
            device_id_type=MESH,
        )

    def rim_copies(base, src, dst):
        return [
            copy(base, src.at[pl.ds(0, H)], dst.at[pl.ds(0, H)], (up, d)),
            copy(base + 1, src.at[pl.ds(H, H)], dst.at[pl.ds(H, H)], (down, d)),
            copy(base + 2, src.at[pl.ds(2 * H, 2 * H)], dst.at[pl.ds(2 * H, 2 * H)], (r, other)),
        ]

    def side_copies(base, src, dst):
        copies = []
        for way, region in ((0, down), (1, up)):
            for e in range(2):
                copies.append((way, e, region))
        return [
            pltpu.make_async_remote_copy(
                src_ref=src[way][e],
                dst_ref=dst.at[2 * (1 - way) + d],
                send_sem=send_sem.at[base + 2 * way + e],
                recv_sem=recv_sem.at[base + 2 * (1 - way) + d],
                device_id=(region, e),
                device_id_type=MESH,
            )
            for way, e, region in copies
        ]

    def side_arrivals(base, src, dst):
        return [copy(base + k, src, dst.at[k], (r, other)) for k in range(4)]

    tile_ref[...] = jnp.zeros_like(tile_ref)
    tile_ref[0:4, 0:H] = send_ref[...].astype(F32)
    lists = tile_ref[...].T
    lane = lax.broadcasted_iota(jnp.int32, (H, F), 1)
    picks = []
    for j in range(4):
        column = lists[0:H, j : j + 1].astype(jnp.int32)
        picks.append((lane == column).astype(F32).astype(BF16))
    rim_pick[...] = jnp.concatenate(picks, axis=0)

    x = x_ref[...]
    x_hi, x_lo = halves(x)
    rim_send[...] = dot(rim_pick[...], x_hi) + dot(rim_pick[...], x_lo)

    pl.semaphore_wait(barrier, 5)
    rims = rim_copies(0, rim_send, rim_recv)
    for c in rims:
        c.start()

    parent = parent_ref[...].reshape(1, F)
    share = share_ref[...].reshape(1, F).astype(F32)
    p_region = lax.shift_right_logical(parent, 8)
    p_local = parent & 255
    at_low = p_region == down
    at_high = p_region == up
    here = p_region == r
    own_hot[...] = one_hot(jnp.where(here, (p_local + C * d) & 255, -1), 2 * C)
    flags = jnp.concatenate(
        [at_low.astype(F32), at_high.astype(F32), jnp.zeros((14, F), F32)], axis=0
    ).astype(BF16)
    before = lax.broadcasted_iota(jnp.int32, (F, F), 0) <= lax.broadcasted_iota(
        jnp.int32, (F, F), 1
    )
    ranks = dot(flags, before.astype(F32).astype(BF16)).astype(jnp.int32) - 1
    side_pick[...] = jnp.concatenate(
        [
            one_hot(jnp.where(at_low, ranks[0:1], -1), SIDE),
            one_hot(jnp.where(at_high, ranks[1:2], -1), SIDE),
        ],
        axis=0,
    )
    sub = lax.broadcasted_iota(jnp.int32, (W, F), 0)
    facts = jnp.where(sub < 64, p_local.astype(F32), share).astype(BF16)
    meta_send[...] = dot_nt(side_pick[...], facts)
    low_meta = meta_send.at[pl.ds(0, SIDE)]
    high_meta = meta_send.at[pl.ds(SIDE, SIDE)]
    metas = side_copies(3, ((low_meta, low_meta), (high_meta, high_meta)), meta_recv)
    for c in metas:
        c.start()
    shares16 = jnp.broadcast_to(share, (16, F)).astype(BF16)
    own_total = dot_nt(shares16, own_hot[...])[0:8]
    tot_send[:, 0:C] = own_total[:, C:]
    tot_send[:, C:] = own_total[:, 0:C]
    tot_copy = copy(7, tot_send, tot_recv, (r, other))
    tot_copy.start()

    tile_ref[0:16, :] = bias_ref[...].reshape(16, W)
    biases = tile_ref[...].T

    def bias(layer, k, centre=False):
        column = biases[:, 4 * layer + k : 4 * layer + k + 1]
        return centred_bias(column) if centre else column

    def prepare(layer):
        for k in range(3):
            wts[6 * layer + k] = stacked(edge_ref[layer, k], centred=k == 2)
            wts[6 * layer + 3 + k] = stacked(node_ref[layer, k], centred=k == 2)

    def fine_layer(layer, rows, rows_split, rim_arrivals, rim_rows):
        own_ref[...] = fold(dot(wts[6 * layer], rows_split)) + bias(layer, 0)
        node_own[...] = fold(dot(wts[6 * layer + 3], rows_split)) + bias(layer, 2)
        src_proj[:, 0:F] = split(fold(dot(wts[6 * layer + 1], rows_split)))
        for c in rim_arrivals:
            c.wait_recv()
        rim = jnp.concatenate(halves(rim_rows[...]), axis=1)
        src_proj[:, F:] = split(fold(dot_nt(wts[6 * layer + 1], rim)))
        total_ref[...] = jnp.zeros_like(total_ref)
        bias1 = jnp.broadcast_to(bias(layer, 1, True), (W, F))

        def slot(s, carry):
            hot = one_hot(nbr_ref[pl.ds(s, 1), :], F + 4 * H)
            gathered = dot(src_proj[...], hot)
            valid = mask_ref[pl.ds(s, 1), :].astype(F32)
            total_ref[...] += message(gathered, own_ref[...], wts[6 * layer + 2], bias1, valid)
            return carry

        lax.fori_loop(0, SLOTS, slot, 0)
        return node_update(
            rows,
            node_own[...],
            total_ref[...],
            wts[6 * layer + 4],
            wts[6 * layer + 5],
            bias(layer, 3, True),
        )

    def coarse_layer(layer, rows, own_split, sources):
        own = fold(dot(wts[6 * layer], own_split)) + bias(layer, 0)
        node_part = fold(dot(wts[6 * layer + 3], own_split)) + bias(layer, 2)
        proj = split(fold(dot(wts[6 * layer + 1], sources())))
        own4 = jnp.concatenate([own] * 4, axis=1)
        bias1 = jnp.broadcast_to(bias(layer, 1, True), (W, 4 * C))
        total = jnp.zeros((W, 4 * C), F32)
        for g in range(4):
            ids = jnp.concatenate([cnbr_ref[4 * g + k : 4 * g + k + 1, :] for k in range(4)], axis=1)
            valid = jnp.concatenate(
                [cmask_ref[4 * g + k : 4 * g + k + 1, :] for k in range(4)], axis=1
            ).astype(F32)
            hot = one_hot((ids + C * d) & 255, 2 * C)
            total += message(dot(proj, hot), own4, wts[6 * layer + 2], bias1, valid)
        total = (total[:, 0:C] + total[:, C : 2 * C]) + (
            total[:, 2 * C : 3 * C] + total[:, 3 * C :]
        )
        return node_update(
            rows,
            node_part,
            total,
            wts[6 * layer + 4],
            wts[6 * layer + 5],
            bias(layer, 3, True),
        )

    prepare(0)
    rows = x.T
    fine_ref[...] = fine_layer(0, rows, split(rows), rims, rim_recv)

    weighted = split(fine_ref[...] * share)
    side_send[...] = fold_lanes(dot_nt(side_pick[...], weighted))
    low_rows = side_send.at[pl.ds(0, SIDE)]
    high_rows = side_send.at[pl.ds(SIDE, SIDE)]
    sides = side_copies(8, ((low_rows, low_rows), (high_rows, high_rows)), side_recv)
    for c in sides:
        c.start()
    partial = fold(dot_nt(weighted, own_hot[...]))
    part_send[:, 0:C] = partial[:, C:]
    part_send[:, C:] = partial[:, 0:C]
    part_copy = copy(12, part_send, part_recv, (r, other))
    part_copy.start()

    prepare(1)
    prepare(2)
    prepare(3)
    for c in side_arrivals(3, low_meta, meta_recv):
        c.wait_recv()
    tot_copy.wait_recv()
    facts_in = meta_recv[...].reshape(4 * SIDE, W)
    p_in = (facts_in[:, 0:1].astype(jnp.int32) + C * d) & 255
    match = lax.broadcasted_iota(jnp.int32, (4 * SIDE, 2 * C), 1) == p_in
    side_hot = match.astype(F32).astype(BF16)
    side_total = jnp.sum(jnp.where(match, facts_in[:, 64:65], 0.0), axis=0, keepdims=True)
    totals = own_total[0:1] + tot_recv[0:1, :] + side_total
    inverse = 1.0 / jnp.maximum(totals, 1.0)

    for c in side_arrivals(8, low_rows, side_recv):
        c.wait_recv()
    from_sides = fold(dot(split(side_recv[...].reshape(4 * SIDE, W).T), side_hot))
    part_copy.wait_recv()
    coarse = (partial + part_recv[...] + from_sides) * inverse

    group = split(coarse)
    mid = coarse_layer(1, coarse[:, 0:C], group[:, 0:C], lambda: group)
    mid_send[...] = mid
    mid_copy = copy(13, mid_send, mid_recv, (r, other))
    mid_copy.start()
    mid_split = split(mid)

    def mid_sources():
        mid_copy.wait_recv()
        return jnp.concatenate([mid_split, split(mid_recv[...])], axis=1)

    coarse_out = coarse_layer(2, mid, mid_split, mid_sources)
    co_split = split(coarse_out)
    reply_send[...] = fold_lanes(dot_nt(side_hot[:, 0:C], co_split)).reshape(4, SIDE, W)
    replies = side_copies(
        14,
        ((reply_send.at[0], reply_send.at[1]), (reply_send.at[2], reply_send.at[3])),
        reply_recv,
    )
    for c in replies:
        c.start()
    co_send[...] = coarse_out
    co_copy = copy(18, co_send, co_recv, (r, other))
    co_copy.start()
    cout_ref[...] = coarse_out.T

    co_copy.wait_recv()
    known = jnp.concatenate([co_split, split(co_recv[...])], axis=1)
    added = fold(dot(known, own_hot[...]))
    for c in side_arrivals(14, reply_send.at[0], reply_recv):
        c.wait_recv()
    back = jnp.concatenate(
        [reply_recv[0] + reply_recv[1], reply_recv[2] + reply_recv[3]], axis=0
    )
    added += fold(dot(split(back.T), side_pick[...]))
    rows = fine_ref[...] + (share * 0.25) * added
    rows_split = split(rows)
    rim2_send[...] = fold_lanes(dot_nt(rim_pick[...], rows_split))
    rims2 = rim_copies(19, rim2_send, rim2_recv)
    for c in rims2:
        c.start()
    out_ref[...] = fine_layer(3, rows, rows_split, rims2, rim2_recv).T

    for c in rims + metas + [tot_copy] + sides + [part_copy, mid_copy] + replies + [co_copy] + rims2:
        c.wait_send()


def body(regions, *args):
    vmem = pl.BlockSpec(memory_space=pltpu.VMEM)
    return pl.pallas_call(
        functools.partial(kernel, regions),
        out_shape=(
            jax.ShapeDtypeStruct((F, W), F32),
            jax.ShapeDtypeStruct((C, W), F32),
        ),
        in_specs=[vmem] * 11,
        out_specs=(vmem, vmem),
        scratch_shapes=[
            pltpu.VMEM((W, W), F32),
            pltpu.VMEM((24, 2 * W, 2 * W), BF16),
            pltpu.VMEM((2 * W, F + 4 * H), BF16),
            pltpu.VMEM((W, F), F32),
            pltpu.VMEM((W, F), F32),
            pltpu.VMEM((W, F), F32),
            pltpu.VMEM((W, F), F32),
            pltpu.VMEM((4 * H, F), BF16),
            pltpu.VMEM((2 * SIDE, F), BF16),
            pltpu.VMEM((2 * C, F), BF16),
            pltpu.VMEM((4 * H, W), F32),
            pltpu.VMEM((4 * H, W), F32),
            pltpu.VMEM((2 * SIDE, W), F32),
            pltpu.VMEM((4, SIDE, W), F32),
            pltpu.VMEM((8, 2 * C), F32),
            pltpu.VMEM((8, 2 * C), F32),
            pltpu.VMEM((W, 2 * C), F32),
            pltpu.VMEM((W, 2 * C), F32),
            pltpu.VMEM((2 * SIDE, W), F32),
            pltpu.VMEM((4, SIDE, W), F32),
            pltpu.VMEM((W, C), F32),
            pltpu.VMEM((W, C), F32),
            pltpu.VMEM((W, C), F32),
            pltpu.VMEM((W, C), F32),
            pltpu.VMEM((4, SIDE, W), F32),
            pltpu.VMEM((4, SIDE, W), F32),
            pltpu.VMEM((4 * H, W), F32),
            pltpu.VMEM((4 * H, W), F32),
            pltpu.SemaphoreType.DMA((22,)),
            pltpu.SemaphoreType.DMA((22,)),
        ],
        compiler_params=pltpu.CompilerParams(collective_id=0, has_side_effects=True),
    )(*args)


def solution(mesh):
    both = ("region", "dom")
    return jax.shard_map(
        functools.partial(body, mesh.shape["region"]),
        mesh=mesh,
        in_specs=(
            P(both, None),
            P(None, both),
            P(None, both),
            P(None, both),
            P(None, both),
            P(None, both),
            P(both),
            P(both),
            P(),
            P(),
            P(),
        ),
        out_specs=(P(both, None), P(both, None)),
        check_vma=False,
    )
```

```python
import functools

import jax
import jax.numpy as jnp
from jax import lax
from jax.experimental import pallas as pl
from jax.experimental.pallas import tpu as pltpu
from jax.sharding import PartitionSpec as P

MESH = pl.DeviceIdType.MESH
EPS = 1e-05
F32 = jnp.float32
BF16 = jnp.bfloat16
W = 128
SLOTS = 16
F = 512
H = 16
C = 128
SIDE = 32


def halves(x):
    hi = x.astype(BF16)
    lo = (x - hi.astype(F32)).astype(BF16)
    return hi, lo


def split(x):
    return jnp.concatenate(halves(x), axis=0)


def dot(a, b):
    return lax.dot_general(a, b, (((1,), (0,)), ((), ())), preferred_element_type=F32)


def dot_nt(a, b):
    return lax.dot_general(a, b, (((1,), (1,)), ((), ())), preferred_element_type=F32)


def fold(y):
    return y[:W] + y[W:]


def fold_lanes(y):
    return y[:, :W] + y[:, W:]


def one_hot(index_row, depth):
    n = index_row.shape[1]
    blocks = []
    for base in range(0, depth, 256):
        size = min(256, depth - base)
        rows = lax.broadcasted_iota(jnp.int32, (size, n), 0).astype(F32).astype(BF16)
        wanted = (index_row - base).astype(F32).astype(BF16)
        blocks.append(jnp.where(rows == wanted, jnp.ones((), BF16), jnp.zeros((), BF16)))
    return blocks[0] if len(blocks) == 1 else jnp.concatenate(blocks, axis=0)


def stacked(w, centred=False):
    t = w.T
    if centred:
        t = t - jnp.sum(t, axis=0, keepdims=True) * (1.0 / W)
    s = split(t)
    return jnp.concatenate([s, s], axis=1)


def scale_of(centred):
    return lax.rsqrt(jnp.sum(centred * centred, axis=0, keepdims=True) * (1.0 / W) + EPS)


def centred_bias(column):
    return column - jnp.sum(column, axis=0, keepdims=True) * (1.0 / W)


def message(hidden, second, second_bias, valid_row):
    hidden = jnp.maximum(hidden, 0.0)
    centred = fold(dot(second, split(hidden))) + second_bias
    return centred * (scale_of(centred) * valid_row)


def node_update(rows, own_part, total, node1, node2, bias3):
    inner = jnp.maximum(own_part + fold(dot(node1, split(total))), 0.0)
    centred = fold(dot(node2, split(inner))) + bias3
    return rows + centred * scale_of(centred)


def kernel(
    regions,
    x_in,
    nbr_in,
    mask_in,
    send_in,
    cnbr_in,
    cmask_in,
    parent_in,
    share_in,
    edge_in,
    node_in,
    bias_in,
    out_ref,
    cout_ref,
    x_ref,
    nbr_ref,
    mask_ref,
    send_ref,
    cnbr_ref,
    cmask_ref,
    parent_ref,
    share_ref,
    edge_ref,
    node_ref,
    bias_ref,
    tile_ref,
    wts,
    base_ref,
    src_proj,
    own_ref,
    node_own,
    total_ref,
    fine_ref,
    rim_pick,
    side_pick,
    own_hot,
    rim_send,
    rim_recv,
    meta_send,
    meta_recv,
    tot_send,
    tot_recv,
    part_send,
    part_recv,
    side_send,
    side_recv,
    mid_send,
    mid_recv,
    co_send,
    co_recv,
    reply_send,
    reply_recv,
    rim2_send,
    rim2_recv,
    send_sem,
    recv_sem,
    load_sem,
):
    r = lax.axis_index("region")
    d = lax.axis_index("dom")
    up = lax.rem(r + 1, regions)
    down = lax.rem(r + regions - 1, regions)
    other = 1 - d
    peers = [(down, 0), (down, 1), (up, 0), (up, 1), (r, other)]
    barrier = pltpu.get_barrier_semaphore()
    for peer in peers:
        pl.semaphore_signal(barrier, inc=1, device_id=peer, device_id_type=MESH)

    loads = [
        pltpu.make_async_copy(src, dst, load_sem.at[k])
        for k, (src, dst) in enumerate(
            (
                (send_in, send_ref),
                (x_in, x_ref),
                (parent_in, parent_ref),
                (share_in, share_ref),
                (edge_in.at[0], edge_ref.at[0]),
                (node_in.at[0], node_ref.at[0]),
                (bias_in, bias_ref),
                (nbr_in, nbr_ref),
                (mask_in, mask_ref),
                (cnbr_in, cnbr_ref),
                (cmask_in, cmask_ref),
                (edge_in.at[pl.ds(1, 3)], edge_ref.at[pl.ds(1, 3)]),
                (node_in.at[pl.ds(1, 3)], node_ref.at[pl.ds(1, 3)]),
            )
        )
    ]
    for c in loads:
        c.start()

    def copy(k, src, dst, peer):
        return pltpu.make_async_remote_copy(
            src_ref=src,
            dst_ref=dst,
            send_sem=send_sem.at[k],
            recv_sem=recv_sem.at[k],
            device_id=peer,
            device_id_type=MESH,
        )

    def rim_copies(base, src, dst):
        return [
            copy(base, src.at[pl.ds(0, H)], dst.at[pl.ds(0, H)], (up, d)),
            copy(base + 1, src.at[pl.ds(H, H)], dst.at[pl.ds(H, H)], (down, d)),
            copy(base + 2, src.at[pl.ds(2 * H, 2 * H)], dst.at[pl.ds(2 * H, 2 * H)], (r, other)),
        ]

    def side_copies(base, src, dst):
        copies = []
        for way, region in ((0, down), (1, up)):
            for e in range(2):
                copies.append((way, e, region))
        return [
            pltpu.make_async_remote_copy(
                src_ref=src[way][e],
                dst_ref=dst.at[2 * (1 - way) + d],
                send_sem=send_sem.at[base + 2 * way + e],
                recv_sem=recv_sem.at[base + 2 * (1 - way) + d],
                device_id=(region, e),
                device_id_type=MESH,
            )
            for way, e, region in copies
        ]

    def side_arrivals(base, src, dst):
        return [copy(base + k, src, dst.at[k], (r, other)) for k in range(4)]

    tile_ref[...] = jnp.zeros_like(tile_ref)
    loads[0].wait()
    tile_ref[0:4, 0:H] = send_ref[...].astype(F32)
    lists = tile_ref[...].T
    lane = lax.broadcasted_iota(jnp.int32, (H, F), 1)
    picks = []
    for j in range(4):
        column = lists[0:H, j : j + 1].astype(jnp.int32)
        picks.append((lane == column).astype(F32).astype(BF16))
    rim_pick[...] = jnp.concatenate(picks, axis=0)

    loads[1].wait()
    x = x_ref[...]
    x_hi, x_lo = halves(x)
    rim_send[...] = dot(rim_pick[...], x_hi) + dot(rim_pick[...], x_lo)

    loads[2].wait()
    loads[3].wait()
    parent = parent_ref[...].reshape(1, F)
    share = share_ref[...].reshape(1, F).astype(F32)
    p_region = lax.shift_right_logical(parent, 8)
    p_local = parent & 255
    at_low = p_region == down
    at_high = p_region == up
    here = p_region == r
    own_hot[...] = one_hot(jnp.where(here, (p_local + C * d) & 255, -1), 2 * C)
    flags = jnp.concatenate(
        [at_low.astype(F32), at_high.astype(F32), jnp.zeros((14, F), F32)], axis=0
    ).astype(BF16)
    before = lax.broadcasted_iota(jnp.int32, (F, F), 0) <= lax.broadcasted_iota(
        jnp.int32, (F, F), 1
    )
    ranks = dot(flags, before.astype(F32).astype(BF16)).astype(jnp.int32) - 1
    side_pick[...] = jnp.concatenate(
        [
            one_hot(jnp.where(at_low, ranks[0:1], -1), SIDE),
            one_hot(jnp.where(at_high, ranks[1:2], -1), SIDE),
        ],
        axis=0,
    )
    sub = lax.broadcasted_iota(jnp.int32, (W, F), 0)
    facts = jnp.where(sub < 64, p_local.astype(F32), share).astype(BF16)
    meta_send[...] = dot_nt(side_pick[...], facts)
    low_meta = meta_send.at[pl.ds(0, SIDE)]
    high_meta = meta_send.at[pl.ds(SIDE, SIDE)]
    metas = side_copies(3, ((low_meta, low_meta), (high_meta, high_meta)), meta_recv)
    shares16 = jnp.broadcast_to(share, (16, F)).astype(BF16)
    own_total = dot_nt(shares16, own_hot[...])[0:8]
    tot_send[:, 0:C] = own_total[:, C:]
    tot_send[:, C:] = own_total[:, 0:C]
    tot_copy = copy(7, tot_send, tot_recv, (r, other))

    pl.semaphore_wait(barrier, 5)
    rims = rim_copies(0, rim_send, rim_recv)
    for c in rims + metas + [tot_copy]:
        c.start()

    for c in loads[4:9]:
        c.wait()
    tile_ref[0:16, :] = bias_ref[...].reshape(16, W)
    biases = tile_ref[...].T

    def bias(layer, k, centre=False):
        column = biases[:, 4 * layer + k : 4 * layer + k + 1]
        return centred_bias(column) if centre else column

    def prepare(layer):
        for k in range(3):
            wts[6 * layer + k] = stacked(edge_ref[layer, k], centred=k == 2)
            wts[6 * layer + 3 + k] = stacked(node_ref[layer, k], centred=k == 2)

    side_twice = jnp.concatenate([side_pick[...], side_pick[...]], axis=0)

    def fine_own(layer, rows_split):
        own_ref[...] = fold(dot(wts[6 * layer], rows_split)) + bias(layer, 0)
        node_own[...] = fold(dot(wts[6 * layer + 3], rows_split)) + bias(layer, 2)
        src_proj[:, 0:F] = split(fold(dot(wts[6 * layer + 1], rows_split)))

        def slot(s, carry):
            hot = one_hot(nbr_ref[pl.ds(s, 1), :], F)
            base_ref[s] = fold(dot(src_proj[:, 0:F], hot)) + own_ref[...]
            return carry

        lax.fori_loop(0, SLOTS, slot, 0, unroll=4)

    def fine_rims(layer, rim_arrivals, rim_rows):
        for c in rim_arrivals:
            c.wait_recv()
        rim = jnp.concatenate(halves(rim_rows[...]), axis=1)
        src_proj[:, F:] = split(fold(dot_nt(wts[6 * layer + 1], rim)))

    def fine_messages(layer, rows):
        total_ref[...] = jnp.zeros_like(total_ref)
        bias1 = jnp.broadcast_to(bias(layer, 1, True), (W, F))

        def slots(g, carry):
            rows4 = [8 * g + k for k in range(8)]
            for t in range(0, F, 256):
                cols = pl.ds(t, 256)
                total = total_ref[:, cols]
                hidden = [
                    base_ref[s, :, cols]
                    + fold(dot(src_proj[:, F:], one_hot(nbr_ref[pl.ds(s, 1), cols] - F, 4 * H)))
                    for s in rows4
                ]
                hidden = [split(jnp.maximum(h, 0.0)) for h in hidden]
                centred = [fold(dot(wts[6 * layer + 2], h)) + bias1[:, 0:256] for h in hidden]
                scales = [
                    scale_of(c) * mask_ref[pl.ds(s, 1), cols].astype(F32) for c, s in zip(centred, rows4)
                ]
                for c, scale in zip(centred, scales):
                    total = total + c * scale
                total_ref[:, cols] = total
            return carry

        lax.fori_loop(0, SLOTS // 8, slots, 0, unroll=1)
        return node_update(
            rows,
            node_own[...],
            total_ref[...],
            wts[6 * layer + 4],
            wts[6 * layer + 5],
            bias(layer, 3, True),
        )

    def picked(values):
        return fold(dot_nt(split(values), side_twice))

    def paired(table):
        parts = jnp.concatenate([table & -16, table & 15], axis=0).astype(F32).astype(BF16)
        both = dot_nt(parts, side_twice)
        values = (both[0:SLOTS] + both[SLOTS:]).astype(jnp.int32)
        first = lax.broadcasted_iota(jnp.int32, (8, W), 1) < 2 * SIDE
        return jnp.where(first, values[0:8], values[8:16])

    def side_nodes(layer, rows):
        ids8 = paired(nbr_ref[...])
        valid8 = paired(mask_ref[...]).astype(F32)
        own4 = jnp.concatenate([picked(own_ref[...])] * 4, axis=1)
        bias1 = jnp.broadcast_to(bias(layer, 1, True), (W, 4 * W))
        total = jnp.zeros((W, 4 * W), F32)
        for g in range(2):
            ids = jnp.concatenate([ids8[4 * g + k : 4 * g + k + 1] for k in range(4)], axis=1)
            valid = jnp.concatenate([valid8[4 * g + k : 4 * g + k + 1] for k in range(4)], axis=1)
            hidden = fold(dot(src_proj[...], one_hot(ids, F + 4 * H))) + own4
            total += message(hidden, wts[6 * layer + 2], bias1, valid)
        total = (total[:, 0:W] + total[:, W : 2 * W]) + (
            total[:, 2 * W : 3 * W] + total[:, 3 * W :]
        )
        total = total + pltpu.roll(total, 2 * SIDE, 1)
        return node_update(
            picked(rows),
            picked(node_own[...]),
            total,
            wts[6 * layer + 4],
            wts[6 * layer + 5],
            bias(layer, 3, True),
        )

    def coarse_layer(layer, rows, own_split, sources):
        own = fold(dot(wts[6 * layer], own_split)) + bias(layer, 0)
        node_part = fold(dot(wts[6 * layer + 3], own_split)) + bias(layer, 2)
        proj = split(fold(dot(wts[6 * layer + 1], sources())))
        own4 = jnp.concatenate([own] * 4, axis=1)
        bias1 = jnp.broadcast_to(bias(layer, 1, True), (W, 4 * C))
        total = jnp.zeros((W, 4 * C), F32)
        for g in range(4):
            ids = jnp.concatenate([cnbr_ref[4 * g + k : 4 * g + k + 1, :] for k in range(4)], axis=1)
            valid = jnp.concatenate(
                [cmask_ref[4 * g + k : 4 * g + k + 1, :] for k in range(4)], axis=1
            ).astype(F32)
            hot = one_hot((ids + C * d) & 255, 2 * C)
            total += message(fold(dot(proj, hot)) + own4, wts[6 * layer + 2], bias1, valid)
        total = (total[:, 0:C] + total[:, C : 2 * C]) + (
            total[:, 2 * C : 3 * C] + total[:, 3 * C :]
        )
        return node_update(
            rows,
            node_part,
            total,
            wts[6 * layer + 4],
            wts[6 * layer + 5],
            bias(layer, 3, True),
        )

    prepare(0)
    rows = x.T
    fine_own(0, split(rows))
    for c in loads[9:]:
        c.wait()
    prepare(1)
    prepare(2)
    prepare(3)
    fine_rims(0, rims, rim_recv)

    side_share = dot_nt(shares16, side_twice)[0:1]
    side_send[...] = (side_nodes(0, rows) * side_share).T[0 : 2 * SIDE]
    low_rows = side_send.at[pl.ds(0, SIDE)]
    high_rows = side_send.at[pl.ds(SIDE, SIDE)]
    sides = side_copies(8, ((low_rows, low_rows), (high_rows, high_rows)), side_recv)
    for c in sides:
        c.start()
    fine_ref[...] = fine_messages(0, rows)

    weighted = split(fine_ref[...] * share)
    partial = fold(dot_nt(weighted, own_hot[...]))
    part_send[:, 0:C] = partial[:, C:]
    part_send[:, C:] = partial[:, 0:C]
    part_copy = copy(12, part_send, part_recv, (r, other))
    part_copy.start()

    for c in side_arrivals(3, low_meta, meta_recv):
        c.wait_recv()
    tot_copy.wait_recv()
    facts_in = meta_recv[...].reshape(4 * SIDE, W)
    p_in = (facts_in[:, 0:1].astype(jnp.int32) + C * d) & 255
    match = lax.broadcasted_iota(jnp.int32, (4 * SIDE, 2 * C), 1) == p_in
    side_hot = match.astype(F32).astype(BF16)
    side_total = jnp.sum(jnp.where(match, facts_in[:, 64:65], 0.0), axis=0, keepdims=True)
    totals = own_total[0:1] + tot_recv[0:1, :] + side_total
    inverse = 1.0 / jnp.maximum(totals, 1.0)

    for c in side_arrivals(8, low_rows, side_recv):
        c.wait_recv()
    from_sides = fold(dot(split(side_recv[...].reshape(4 * SIDE, W).T), side_hot))
    part_copy.wait_recv()
    coarse = (partial + part_recv[...] + from_sides) * inverse

    group = split(coarse)
    mid = coarse_layer(1, coarse[:, 0:C], group[:, 0:C], lambda: group)
    mid_send[...] = mid
    mid_copy = copy(13, mid_send, mid_recv, (r, other))
    mid_copy.start()
    mid_split = split(mid)

    def mid_sources():
        mid_copy.wait_recv()
        return jnp.concatenate([mid_split, split(mid_recv[...])], axis=1)

    coarse_out = coarse_layer(2, mid, mid_split, mid_sources)
    co_split = split(coarse_out)
    reply_send[...] = fold_lanes(dot_nt(side_hot[:, 0:C], co_split)).reshape(4, SIDE, W)
    replies = side_copies(
        14,
        ((reply_send.at[0], reply_send.at[1]), (reply_send.at[2], reply_send.at[3])),
        reply_recv,
    )
    for c in replies:
        c.start()
    co_send[...] = coarse_out
    co_copy = copy(18, co_send, co_recv, (r, other))
    co_copy.start()
    cout_ref[...] = coarse_out.T

    co_copy.wait_recv()
    known = jnp.concatenate([co_split, split(co_recv[...])], axis=1)
    added = fold(dot(known, own_hot[...]))
    for c in side_arrivals(14, reply_send.at[0], reply_recv):
        c.wait_recv()
    back = jnp.concatenate(
        [reply_recv[0] + reply_recv[1], reply_recv[2] + reply_recv[3]], axis=0
    )
    added += fold(dot(split(back.T), side_pick[...]))
    rows = fine_ref[...] + (share * 0.25) * added
    rows_split = split(rows)
    rim2_send[...] = fold_lanes(dot_nt(rim_pick[...], rows_split))
    rims2 = rim_copies(19, rim2_send, rim2_recv)
    for c in rims2:
        c.start()
    fine_own(3, rows_split)
    fine_rims(3, rims2, rim2_recv)
    out_ref[...] = fine_messages(3, rows).T

    for c in rims + metas + [tot_copy] + sides + [part_copy, mid_copy] + replies + [co_copy] + rims2:
        c.wait_send()


def body(regions, *args):
    vmem = pl.BlockSpec(memory_space=pltpu.VMEM)
    return pl.pallas_call(
        functools.partial(kernel, regions),
        out_shape=(
            jax.ShapeDtypeStruct((F, W), F32),
            jax.ShapeDtypeStruct((C, W), F32),
        ),
        in_specs=[pl.BlockSpec(memory_space=pl.ANY)] * 11,
        out_specs=(vmem, vmem),
        scratch_shapes=[pltpu.VMEM(a.shape, a.dtype) for a in args]
        + [
            pltpu.VMEM((W, W), F32),
            pltpu.VMEM((24, 2 * W, 2 * W), BF16),
            pltpu.VMEM((SLOTS, W, F), F32),
            pltpu.VMEM((2 * W, F + 4 * H), BF16),
            pltpu.VMEM((W, F), F32),
            pltpu.VMEM((W, F), F32),
            pltpu.VMEM((W, F), F32),
            pltpu.VMEM((W, F), F32),
            pltpu.VMEM((4 * H, F), BF16),
            pltpu.VMEM((2 * SIDE, F), BF16),
            pltpu.VMEM((2 * C, F), BF16),
            pltpu.VMEM((4 * H, W), F32),
            pltpu.VMEM((4 * H, W), F32),
            pltpu.VMEM((2 * SIDE, W), F32),
            pltpu.VMEM((4, SIDE, W), F32),
            pltpu.VMEM((8, 2 * C), F32),
            pltpu.VMEM((8, 2 * C), F32),
            pltpu.VMEM((W, 2 * C), F32),
            pltpu.VMEM((W, 2 * C), F32),
            pltpu.VMEM((2 * SIDE, W), F32),
            pltpu.VMEM((4, SIDE, W), F32),
            pltpu.VMEM((W, C), F32),
            pltpu.VMEM((W, C), F32),
            pltpu.VMEM((W, C), F32),
            pltpu.VMEM((W, C), F32),
            pltpu.VMEM((4, SIDE, W), F32),
            pltpu.VMEM((4, SIDE, W), F32),
            pltpu.VMEM((4 * H, W), F32),
            pltpu.VMEM((4 * H, W), F32),
            pltpu.SemaphoreType.DMA((22,)),
            pltpu.SemaphoreType.DMA((22,)),
            pltpu.SemaphoreType.DMA((13,)),
        ],
        compiler_params=pltpu.CompilerParams(collective_id=0, has_side_effects=True),
    )(*args)


def solution(mesh):
    both = ("region", "dom")
    return jax.shard_map(
        functools.partial(body, mesh.shape["region"]),
        mesh=mesh,
        in_specs=(
            P(both, None),
            P(None, both),
            P(None, both),
            P(None, both),
            P(None, both),
            P(None, both),
            P(both),
            P(both),
            P(),
            P(),
            P(),
        ),
        out_specs=(P(both, None), P(both, None)),
        check_vma=False,
    )
```

```python
import functools

import jax
import jax.numpy as jnp
from jax import lax
from jax.experimental import pallas as pl
from jax.experimental.pallas import tpu as pltpu
from jax.sharding import PartitionSpec as P

MESH = pl.DeviceIdType.MESH
EPS = 1e-05
F32 = jnp.float32
BF16 = jnp.bfloat16
W = 128
SLOTS = 16
F = 512
H = 16
C = 128
SIDE = 32


def halves(x):
    hi = x.astype(BF16)
    lo = (x - hi.astype(F32)).astype(BF16)
    return hi, lo


def split(x):
    return jnp.concatenate(halves(x), axis=0)


def dot(a, b):
    return lax.dot_general(a, b, (((1,), (0,)), ((), ())), preferred_element_type=F32)


def dot_nt(a, b):
    return lax.dot_general(a, b, (((1,), (1,)), ((), ())), preferred_element_type=F32)


def fold(y):
    return y[:W] + y[W:]


def fold_lanes(y):
    return y[:, :W] + y[:, W:]


def one_hot(index_row, depth):
    n = index_row.shape[1]
    blocks = []
    for base in range(0, depth, 256):
        size = min(256, depth - base)
        rows = lax.broadcasted_iota(jnp.int32, (size, n), 0).astype(F32).astype(BF16)
        wanted = (index_row - base).astype(F32).astype(BF16)
        blocks.append(jnp.where(rows == wanted, jnp.ones((), BF16), jnp.zeros((), BF16)))
    return blocks[0] if len(blocks) == 1 else jnp.concatenate(blocks, axis=0)


def stacked(w, centred=False):
    t = w.T
    if centred:
        t = t - jnp.sum(t, axis=0, keepdims=True) * (1.0 / W)
    s = split(t)
    return jnp.concatenate([s, s], axis=1)


def scale_of(centred):
    return lax.rsqrt(jnp.sum(centred * centred, axis=0, keepdims=True) * (1.0 / W) + EPS)


def centred_bias(column):
    return column - jnp.sum(column, axis=0, keepdims=True) * (1.0 / W)


def message(hidden, second, second_bias, valid_row):
    hidden = jnp.maximum(hidden, 0.0)
    centred = fold(dot(second, split(hidden))) + second_bias
    return centred * (scale_of(centred) * valid_row)


def node_update(rows, own_part, total, node1, node2, bias3):
    inner = jnp.maximum(own_part + fold(dot(node1, split(total))), 0.0)
    centred = fold(dot(node2, split(inner))) + bias3
    return rows + centred * scale_of(centred)


def kernel(
    regions,
    x_in,
    nbr_in,
    mask_in,
    send_in,
    cnbr_in,
    cmask_in,
    parent_in,
    share_in,
    edge_in,
    node_in,
    bias_in,
    out_ref,
    cout_ref,
    x_ref,
    nbr_ref,
    mask_ref,
    send_ref,
    cnbr_ref,
    cmask_ref,
    parent_ref,
    share_ref,
    edge_ref,
    node_ref,
    bias_ref,
    tile_ref,
    wts,
    base_ref,
    src_proj,
    own_ref,
    node_own,
    total_ref,
    fine_ref,
    pick_all,
    own_hot,
    side_ids,
    rim_send,
    rim_recv,
    meta_send,
    meta_recv,
    tot_send,
    tot_recv,
    part_send,
    part_recv,
    side_send,
    side_recv,
    mid_send,
    mid_recv,
    co_send,
    co_recv,
    pay_send,
    pay_recv,
    rim2_send,
    rim2_recv,
    send_sem,
    recv_sem,
    load_sem,
):
    r = lax.axis_index("region")
    d = lax.axis_index("dom")
    up = lax.rem(r + 1, regions)
    down = lax.rem(r + regions - 1, regions)
    other = 1 - d
    up2 = lax.rem(r + 2, regions)
    down2 = lax.rem(r + regions - 2, regions)
    peers = [(down, d), (down, other), (up, d), (up, other), (r, other), (up2, d), (down2, d)]
    barrier = pltpu.get_barrier_semaphore()
    for peer in peers:
        pl.semaphore_signal(barrier, inc=1, device_id=peer, device_id_type=MESH)

    loads = [
        pltpu.make_async_copy(src, dst, load_sem.at[k])
        for k, (src, dst) in enumerate(
            (
                (send_in, send_ref),
                (x_in, x_ref),
                (parent_in, parent_ref),
                (share_in, share_ref),
                (edge_in.at[0], edge_ref.at[0]),
                (node_in.at[0], node_ref.at[0]),
                (bias_in, bias_ref),
                (nbr_in, nbr_ref),
                (mask_in, mask_ref),
                (cnbr_in, cnbr_ref),
                (cmask_in, cmask_ref),
                (edge_in.at[pl.ds(1, 3)], edge_ref.at[pl.ds(1, 3)]),
                (node_in.at[pl.ds(1, 3)], node_ref.at[pl.ds(1, 3)]),
            )
        )
    ]
    for c in loads:
        c.start()

    def copy(k, src, dst, peer):
        return pltpu.make_async_remote_copy(
            src_ref=src,
            dst_ref=dst,
            send_sem=send_sem.at[k],
            recv_sem=recv_sem.at[k],
            device_id=peer,
            device_id_type=MESH,
        )

    def rim_copies(base, src, dst):
        return [
            copy(base, src.at[pl.ds(0, H)], dst.at[pl.ds(0, H)], (up, d)),
            copy(base + 1, src.at[pl.ds(H, H)], dst.at[pl.ds(H, H)], (down, d)),
            copy(base + 2, src.at[pl.ds(2 * H, 2 * H)], dst.at[pl.ds(2 * H, 2 * H)], (r, other)),
        ]

    def four_copies(base, low, high, dst):
        return [
            pltpu.make_async_remote_copy(
                src_ref=src,
                dst_ref=dst.at[2 * (1 - way) + cross],
                send_sem=send_sem.at[base + 2 * way + cross],
                recv_sem=recv_sem.at[base + 2 * (1 - way) + cross],
                device_id=(region, other if cross else d),
                device_id_type=MESH,
            )
            for way, src, region in ((0, low, down), (1, high, up))
            for cross in range(2)
        ]

    def four_arrivals(base, src, dst):
        return [copy(base + k, src, dst.at[k], (r, other)) for k in range(4)]

    tile_ref[...] = jnp.zeros_like(tile_ref)
    loads[0].wait()
    tile_ref[0:4, 0:H] = send_ref[...].astype(F32)
    lists = tile_ref[...].T
    lane = lax.broadcasted_iota(jnp.int32, (H, F), 1)
    picks = []
    for j in range(4):
        column = lists[0:H, j : j + 1].astype(jnp.int32)
        picks.append((lane == column).astype(F32).astype(BF16))
    pick_all[2 * SIDE :, :] = jnp.concatenate(picks, axis=0)

    loads[1].wait()
    x = x_ref[...]
    x_hi, x_lo = halves(x)
    rim_send[...] = dot(pick_all[2 * SIDE :, :], x_hi) + dot(pick_all[2 * SIDE :, :], x_lo)

    loads[2].wait()
    loads[3].wait()
    parent = parent_ref[...].reshape(1, F)
    share = share_ref[...].reshape(1, F).astype(F32)
    p_region = lax.shift_right_logical(parent, 8)
    p_local = parent & 255
    at_low = p_region == down
    at_high = p_region == up
    here = p_region == r
    own_hot[...] = one_hot(jnp.where(here, (p_local + C * d) & 255, -1), 2 * C)
    flags = jnp.concatenate(
        [at_low.astype(F32), at_high.astype(F32), jnp.zeros((14, F), F32)], axis=0
    ).astype(BF16)
    before = lax.broadcasted_iota(jnp.int32, (F, F), 0) <= lax.broadcasted_iota(
        jnp.int32, (F, F), 1
    )
    ranks = dot(flags, before.astype(F32).astype(BF16)).astype(jnp.int32) - 1
    low_rank = jnp.where(at_low, ranks[0:1], -1)
    high_rank = jnp.where(at_high, ranks[1:2], -1)
    pick_all[0 : 2 * SIDE, :] = jnp.concatenate(
        [one_hot(low_rank, SIDE), one_hot(high_rank, SIDE)], axis=0
    )
    side_pick = pick_all.at[pl.ds(0, 2 * SIDE)]
    rim_pick = pick_all.at[pl.ds(2 * SIDE, 4 * H)]
    number = jnp.where(at_high, high_rank + SIDE, low_rank) + 1
    src_proj[2 * W :, 0:F] = jnp.broadcast_to(number.astype(F32), (16, F)).astype(BF16)
    where_at = at_low.astype(F32) + 2.0 * at_high.astype(F32)
    facts = jnp.concatenate(
        [p_local.astype(F32), share, where_at, jnp.zeros((13, F), F32)], axis=0
    ).astype(BF16)
    meta_send[...] = dot_nt(facts, pick_all[...])[0:8]
    metas = four_copies(3, meta_send, meta_send, meta_recv)
    metas.append(copy(7, meta_send, meta_recv.at[4], (r, other)))
    shares16 = jnp.broadcast_to(share, (16, F)).astype(BF16)
    own_total = dot_nt(shares16, own_hot[...])[0:8]
    tot_send[:, 0:C] = own_total[:, C:]
    tot_send[:, C:] = own_total[:, 0:C]
    tot_copy = copy(8, tot_send, tot_recv, (r, other))

    pl.semaphore_wait(barrier, 7)
    rims = rim_copies(0, rim_send, rim_recv)
    for c in rims + metas + [tot_copy]:
        c.start()

    for c in loads[4:9]:
        c.wait()
    tile_ref[0:16, :] = bias_ref[...].reshape(16, W)
    biases = tile_ref[...].T

    def bias(layer, k, centre=False):
        column = biases[:, 4 * layer + k : 4 * layer + k + 1]
        return centred_bias(column) if centre else column

    def prepare(layer):
        for k in range(3):
            wts[6 * layer + k] = stacked(edge_ref[layer, k], centred=k == 2)
            wts[6 * layer + 3 + k] = stacked(node_ref[layer, k], centred=k == 2)

    side_twice = jnp.concatenate([side_pick[...], side_pick[...]], axis=0)

    def fine_own(layer, rows_split):
        own_ref[...] = fold(dot(wts[6 * layer], rows_split)) + bias(layer, 0)
        node_own[...] = fold(dot(wts[6 * layer + 3], rows_split)) + bias(layer, 2)
        src_proj[0 : 2 * W, 0:F] = split(fold(dot(wts[6 * layer + 1], rows_split)))

        def slot(s, carry):
            hot = one_hot(nbr_ref[pl.ds(s, 1), :], F)
            if layer == 0:
                gathered = dot(src_proj[:, 0:F], hot)
                side_ids[pl.ds(s, 1), :] = gathered[2 * W : 2 * W + 1].astype(jnp.int32) - 1
            else:
                gathered = dot(src_proj[0 : 2 * W, 0:F], hot)
            base_ref[s] = fold(gathered[0 : 2 * W]) + own_ref[...]
            return carry

        lax.fori_loop(0, SLOTS, slot, 0, unroll=4)

    def fine_rims(layer, rim_arrivals, rim_rows):
        for c in rim_arrivals:
            c.wait_recv()
        rim = jnp.concatenate(halves(rim_rows[...]), axis=1)
        src_proj[0 : 2 * W, F:] = split(fold(dot_nt(wts[6 * layer + 1], rim)))

    def fine_messages(layer, rows, extra_proj, extra_hot):
        total_ref[...] = jnp.zeros_like(total_ref)
        bias1 = jnp.broadcast_to(bias(layer, 1, True), (W, F))

        def slots(g, carry):
            rows4 = [8 * g + k for k in range(8)]
            for t in range(0, F, 256):
                cols = pl.ds(t, 256)
                total = total_ref[:, cols]
                hidden = [
                    base_ref[s, :, cols]
                    + fold(dot(extra_proj, extra_hot(s, cols)))
                    for s in rows4
                ]
                hidden = [split(jnp.maximum(h, 0.0)) for h in hidden]
                centred = [fold(dot(wts[6 * layer + 2], h)) + bias1[:, 0:256] for h in hidden]
                scales = [
                    scale_of(c) * mask_ref[pl.ds(s, 1), cols].astype(F32) for c, s in zip(centred, rows4)
                ]
                for c, scale in zip(centred, scales):
                    total = total + c * scale
                total_ref[:, cols] = total
            return carry

        lax.fori_loop(0, SLOTS // 8, slots, 0, unroll=1)
        return node_update(
            rows,
            node_own[...],
            total_ref[...],
            wts[6 * layer + 4],
            wts[6 * layer + 5],
            bias(layer, 3, True),
        )

    def picked(values):
        return fold(dot_nt(split(values), side_twice))

    def paired(table):
        parts = jnp.concatenate([table & -16, table & 15], axis=0).astype(F32).astype(BF16)
        both = dot_nt(parts, side_twice)
        values = (both[0:SLOTS] + both[SLOTS:]).astype(jnp.int32)
        first = lax.broadcasted_iota(jnp.int32, (8, W), 1) < 2 * SIDE
        return jnp.where(first, values[0:8], values[8:16])

    def side_nodes(layer, rows):
        ids8 = paired(nbr_ref[...])
        valid8 = paired(mask_ref[...]).astype(F32)
        own4 = jnp.concatenate([picked(own_ref[...])] * 4, axis=1)
        bias1 = jnp.broadcast_to(bias(layer, 1, True), (W, 4 * W))
        total = jnp.zeros((W, 4 * W), F32)
        for g in range(2):
            ids = jnp.concatenate([ids8[4 * g + k : 4 * g + k + 1] for k in range(4)], axis=1)
            valid = jnp.concatenate([valid8[4 * g + k : 4 * g + k + 1] for k in range(4)], axis=1)
            hidden = fold(dot(src_proj[0 : 2 * W, :], one_hot(ids, F + 4 * H))) + own4
            total += message(hidden, wts[6 * layer + 2], bias1, valid)
        total = (total[:, 0:W] + total[:, W : 2 * W]) + (
            total[:, 2 * W : 3 * W] + total[:, 3 * W :]
        )
        total = total + pltpu.roll(total, 2 * SIDE, 1)
        return node_update(
            picked(rows),
            picked(node_own[...]),
            total,
            wts[6 * layer + 4],
            wts[6 * layer + 5],
            bias(layer, 3, True),
        )

    def coarse_layer(layer, rows, own_split, sources):
        own = fold(dot(wts[6 * layer], own_split)) + bias(layer, 0)
        node_part = fold(dot(wts[6 * layer + 3], own_split)) + bias(layer, 2)
        proj = split(fold(dot(wts[6 * layer + 1], sources())))
        own4 = jnp.concatenate([own] * 4, axis=1)
        bias1 = jnp.broadcast_to(bias(layer, 1, True), (W, 4 * C))
        id_rows, valid_rows = [], []
        for g in range(4):
            k = range(4 * g, 4 * g + 4)
            id_rows.append(jnp.concatenate([cnbr_ref[i : i + 1, :] for i in k], axis=1))
            valid_rows.append(
                jnp.concatenate([cmask_ref[i : i + 1, :] for i in k], axis=1).astype(F32)
            )
        hots = [one_hot((ids + C * d) & 255, 2 * C) for ids in id_rows]
        hidden = [split(jnp.maximum(fold(dot(proj, hot)) + own4, 0.0)) for hot in hots]
        centred = [fold(dot(wts[6 * layer + 2], h)) + bias1 for h in hidden]
        scales = [scale_of(c) * valid for c, valid in zip(centred, valid_rows)]
        total = centred[0] * scales[0] + centred[1] * scales[1]
        total = total + (centred[2] * scales[2] + centred[3] * scales[3])
        total = (total[:, 0:C] + total[:, C : 2 * C]) + (
            total[:, 2 * C : 3 * C] + total[:, 3 * C :]
        )
        return node_update(
            rows,
            node_part,
            total,
            wts[6 * layer + 4],
            wts[6 * layer + 5],
            bias(layer, 3, True),
        )

    prepare(0)
    rows = x.T
    fine_own(0, split(rows))
    for c in loads[9:]:
        c.wait()
    prepare(1)
    prepare(2)
    prepare(3)
    fine_rims(0, rims, rim_recv)

    side_share = dot_nt(shares16, side_twice)[0:1]
    side_send[...] = (side_nodes(0, rows) * side_share).T[0 : 2 * SIDE]
    low_rows = side_send.at[pl.ds(0, SIDE)]
    high_rows = side_send.at[pl.ds(SIDE, SIDE)]
    sides = four_copies(9, low_rows, high_rows, side_recv)
    for c in sides:
        c.start()
    def rim_hot(s, cols):
        return one_hot(nbr_ref[pl.ds(s, 1), cols] - F, 4 * H)

    fine_ref[...] = fine_messages(0, rows, src_proj[0 : 2 * W, F:], rim_hot)

    weighted = split(fine_ref[...] * share)
    partial = fold(dot_nt(weighted, own_hot[...]))
    part_send[:, 0:C] = partial[:, C:]
    part_send[:, C:] = partial[:, 0:C]
    part_copy = copy(13, part_send, part_recv, (r, other))
    part_copy.start()

    rim2_send[...] = fold_lanes(dot_nt(rim_pick[...], split(fine_ref[...])))
    rims2 = rim_copies(20, rim2_send, rim2_recv)
    for c in rims2:
        c.start()

    for c in four_arrivals(3, meta_send, meta_recv) + metas[4:]:
        c.wait_recv()
    tile_ref[0:40, :] = meta_recv[...].reshape(40, W)
    tile_ref[40:48, :] = meta_send[...]
    lists = tile_ref[...].T

    def listed(k, start, size, only=None):
        rows_at = slice(start, start + size)
        weight = lists[rows_at, 8 * k + 1 : 8 * k + 2]
        if only is not None:
            weight = jnp.where(lists[rows_at, 8 * k + 2 : 8 * k + 3] == only, weight, 0.0)
        return lists[rows_at, 8 * k : 8 * k + 1], weight

    def chosen(entries):
        wanted = jnp.concatenate([e[0] for e in entries], axis=0).astype(jnp.int32)
        weight = jnp.concatenate([e[1] for e in entries], axis=0)
        nodes = lax.broadcasted_iota(jnp.int32, (wanted.shape[0], 2 * C), 1)
        return nodes == ((wanted + C * d) & 255), weight

    match, weight_in = chosen(
        [listed(0, 32, 32), listed(1, 32, 32), listed(2, 0, 32), listed(3, 0, 32)]
    )
    side_hot = match.astype(F32).astype(BF16)
    side_total = jnp.sum(jnp.where(match, weight_in, 0.0), axis=0, keepdims=True)
    match, weight_out = chosen(
        [listed(2, 0, 32), listed(3, 96, 32, 1.0), listed(5, 64, 16, 0.0)]
        + [listed(0, 32, 32), listed(1, 96, 32, 2.0), listed(5, 80, 16, 0.0)]
        + [listed(2, 64, 16, 1.0), listed(0, 80, 16, 2.0)]
        + [listed(0, 64, 16, 2.0), listed(2, 80, 16, 1.0), listed(4, 96, 32, 0.0)]
    )
    out_hot = jnp.where(match, weight_out * 0.25, 0.0).astype(BF16)
    tot_copy.wait_recv()
    totals = own_total[0:1] + tot_recv[0:1, :] + side_total
    inverse = 1.0 / jnp.maximum(totals, 1.0)

    for c in four_arrivals(9, low_rows, side_recv):
        c.wait_recv()
    from_sides = fold(dot(split(side_recv[...].reshape(4 * SIDE, W).T), side_hot))
    part_copy.wait_recv()
    coarse = (partial + part_recv[...] + from_sides) * inverse

    group = split(coarse)
    mid = coarse_layer(1, coarse[:, 0:C], group[:, 0:C], lambda: group)
    mid_send[...] = mid
    mid_copy = copy(14, mid_send, mid_recv, (r, other))
    mid_copy.start()
    mid_split = split(mid)

    def mid_sources():
        mid_copy.wait_recv()
        return jnp.concatenate([mid_split, split(mid_recv[...])], axis=1)

    coarse_out = coarse_layer(2, mid, mid_split, mid_sources)
    co_split = split(coarse_out)
    co_send[...] = coarse_out
    co_copy = copy(15, co_send, co_recv, (r, other))
    co_copy.start()
    cout_ref[...] = coarse_out.T

    co_copy.wait_recv()
    known = jnp.concatenate([co_split, split(co_recv[...])], axis=1)
    given = fold_lanes(dot_nt(out_hot, known))
    pay_send[...] = given[0:192]
    pays = [
        copy(
            16 + k,
            pay_send.at[pl.ds(start, size)],
            pay_recv.at[pl.ds(start, size)],
            (region, d),
        )
        for k, (start, size, region) in enumerate(
            ((0, 80, up), (80, 80, down), (160, 16, up2), (176, 16, down2))
        )
    ]
    for c in pays:
        c.start()
    rows = fine_ref[...] + (share * 0.25) * fold(dot(known, own_hot[...]))
    fine_own(3, split(rows))

    for c in rims2 + pays:
        c.wait_recv()
    from_low, from_high = pay_recv[0:32, :], pay_recv[80:112, :]
    rim = rim2_recv[...] + given[192:256]
    rim += jnp.concatenate(
        [
            pay_recv[64:80, :] + pay_recv[160:176, :],
            pay_recv[144:160, :] + pay_recv[176:192, :],
            pay_recv[32:64, :] + pay_recv[112:144, :],
        ],
        axis=0,
    )
    late = jnp.concatenate([rim, from_low, from_high], axis=0)
    late_split = split(late.T)
    side_split = late_split[:, 4 * H :]
    extra = jnp.concatenate(
        [split(fold(dot(wts[19], late_split))), split(fold(dot(wts[18], side_split)))], axis=1
    )
    rows += fold(dot(side_split, side_pick[...]))
    node_own[...] += fold(dot(split(fold(dot(wts[21], side_split))), side_pick[...]))

    def late_hot(s, cols):
        return jnp.concatenate(
            [
                one_hot(nbr_ref[pl.ds(s, 1), cols] - F, 4 * H),
                one_hot(side_ids[pl.ds(s, 1), cols], 2 * SIDE),
                side_pick[:, cols],
            ],
            axis=0,
        )

    out_ref[...] = fine_messages(3, rows, extra, late_hot).T

    sent = rims + metas + [tot_copy] + sides + [part_copy, mid_copy, co_copy] + pays + rims2
    for c in sent:
        c.wait_send()


def body(regions, *args):
    vmem = pl.BlockSpec(memory_space=pltpu.VMEM)
    return pl.pallas_call(
        functools.partial(kernel, regions),
        out_shape=(
            jax.ShapeDtypeStruct((F, W), F32),
            jax.ShapeDtypeStruct((C, W), F32),
        ),
        in_specs=[pl.BlockSpec(memory_space=pl.ANY)] * 11,
        out_specs=(vmem, vmem),
        scratch_shapes=[pltpu.VMEM(a.shape, a.dtype) for a in args]
        + [
            pltpu.VMEM((W, W), F32),
            pltpu.VMEM((24, 2 * W, 2 * W), BF16),
            pltpu.VMEM((SLOTS, W, F), F32),
            pltpu.VMEM((2 * W + 16, F + 4 * H), BF16),
            pltpu.VMEM((W, F), F32),
            pltpu.VMEM((W, F), F32),
            pltpu.VMEM((W, F), F32),
            pltpu.VMEM((W, F), F32),
            pltpu.VMEM((2 * SIDE + 4 * H, F), BF16),
            pltpu.VMEM((2 * C, F), BF16),
            pltpu.VMEM((SLOTS, F), jnp.int32),
            pltpu.VMEM((4 * H, W), F32),
            pltpu.VMEM((4 * H, W), F32),
            pltpu.VMEM((8, W), F32),
            pltpu.VMEM((5, 8, W), F32),
            pltpu.VMEM((8, 2 * C), F32),
            pltpu.VMEM((8, 2 * C), F32),
            pltpu.VMEM((W, 2 * C), F32),
            pltpu.VMEM((W, 2 * C), F32),
            pltpu.VMEM((2 * SIDE, W), F32),
            pltpu.VMEM((4, SIDE, W), F32),
            pltpu.VMEM((W, C), F32),
            pltpu.VMEM((W, C), F32),
            pltpu.VMEM((W, C), F32),
            pltpu.VMEM((W, C), F32),
            pltpu.VMEM((192, W), F32),
            pltpu.VMEM((192, W), F32),
            pltpu.VMEM((4 * H, W), F32),
            pltpu.VMEM((4 * H, W), F32),
            pltpu.SemaphoreType.DMA((23,)),
            pltpu.SemaphoreType.DMA((23,)),
            pltpu.SemaphoreType.DMA((13,)),
        ],
        compiler_params=pltpu.CompilerParams(collective_id=0, has_side_effects=True),
    )(*args)


def solution(mesh):
    both = ("region", "dom")
    return jax.shard_map(
        functools.partial(body, mesh.shape["region"]),
        mesh=mesh,
        in_specs=(
            P(both, None),
            P(None, both),
            P(None, both),
            P(None, both),
            P(None, both),
            P(None, both),
            P(both),
            P(both),
            P(),
            P(),
            P(),
        ),
        out_specs=(P(both, None), P(both, None)),
        check_vma=False,
    )
```

```python
import functools

import jax
import jax.numpy as jnp
from jax import lax
from jax.experimental import pallas as pl
from jax.experimental.pallas import tpu as pltpu
from jax.sharding import PartitionSpec as P

MESH = pl.DeviceIdType.MESH
EPS = 1e-05
F32 = jnp.float32
BF16 = jnp.bfloat16
W = 128
SLOTS = 16
F = 512
H = 16
C = 128
SIDE = 32


def halves(x):
    hi = x.astype(BF16)
    lo = (x - hi.astype(F32)).astype(BF16)
    return hi, lo


def split(x):
    return jnp.concatenate(halves(x), axis=0)


def dot(a, b):
    return lax.dot_general(a, b, (((1,), (0,)), ((), ())), preferred_element_type=F32)


def dot_nt(a, b):
    return lax.dot_general(a, b, (((1,), (1,)), ((), ())), preferred_element_type=F32)


def fold(y):
    return y[:W] + y[W:]


def fold_lanes(y):
    return y[:, :W] + y[:, W:]


def one_hot(index_row, depth):
    n = index_row.shape[1]
    blocks = []
    for base in range(0, depth, 256):
        size = min(256, depth - base)
        rows = lax.broadcasted_iota(jnp.int32, (size, n), 0).astype(F32).astype(BF16)
        wanted = (index_row - base).astype(F32).astype(BF16)
        blocks.append(jnp.where(rows == wanted, jnp.ones((), BF16), jnp.zeros((), BF16)))
    return blocks[0] if len(blocks) == 1 else jnp.concatenate(blocks, axis=0)


def stacked(w, centred=False):
    t = w.T
    if centred:
        t = t - jnp.sum(t, axis=0, keepdims=True) * (1.0 / W)
    s = split(t)
    return jnp.concatenate([s, s], axis=1)


def scale_of(centred):
    return lax.rsqrt(jnp.sum(centred * centred, axis=0, keepdims=True) * (1.0 / W) + EPS)


def centred_bias(column):
    return column - jnp.sum(column, axis=0, keepdims=True) * (1.0 / W)


def message(hidden, second, second_bias, valid_row):
    hidden = jnp.maximum(hidden, 0.0)
    centred = fold(dot(second, split(hidden))) + second_bias
    return centred * (scale_of(centred) * valid_row)


def node_update(rows, own_part, total, node1, node2, bias3):
    inner = jnp.maximum(own_part + fold(dot(node1, split(total))), 0.0)
    centred = fold(dot(node2, split(inner))) + bias3
    return rows + centred * scale_of(centred)


def kernel(
    regions,
    x_in,
    nbr_in,
    mask_in,
    send_in,
    cnbr_in,
    cmask_in,
    parent_in,
    share_in,
    edge_in,
    node_in,
    bias_in,
    out_ref,
    cout_ref,
    x_ref,
    nbr_ref,
    mask_ref,
    send_ref,
    cnbr_ref,
    cmask_ref,
    parent_ref,
    share_ref,
    edge_ref,
    node_ref,
    bias_ref,
    tile_ref,
    wts,
    base_ref,
    src_proj,
    own_ref,
    node_own,
    total_ref,
    fine_ref,
    pick_all,
    own_hot,
    side_ids,
    rim_send,
    rim_recv,
    meta_send,
    meta_recv,
    tot_send,
    tot_recv,
    part_send,
    part_recv,
    side_send,
    side_recv,
    mid_send,
    mid_recv,
    co_send,
    co_recv,
    pay_send,
    pay_recv,
    rim2_send,
    rim2_recv,
    send_sem,
    recv_sem,
    load_sem,
):
    r = lax.axis_index("region")
    d = lax.axis_index("dom")
    up = lax.rem(r + 1, regions)
    down = lax.rem(r + regions - 1, regions)
    other = 1 - d
    up2 = lax.rem(r + 2, regions)
    down2 = lax.rem(r + regions - 2, regions)
    peers = [(down, d), (down, other), (up, d), (up, other), (r, other), (up2, d), (down2, d)]
    barrier = pltpu.get_barrier_semaphore()
    for peer in peers:
        pl.semaphore_signal(barrier, inc=1, device_id=peer, device_id_type=MESH)

    loads = [
        pltpu.make_async_copy(src, dst, load_sem.at[k])
        for k, (src, dst) in enumerate(
            (
                (send_in, send_ref),
                (x_in, x_ref),
                (parent_in, parent_ref),
                (share_in, share_ref),
                (edge_in.at[0], edge_ref.at[0]),
                (node_in.at[0], node_ref.at[0]),
                (bias_in, bias_ref),
                (nbr_in, nbr_ref),
                (mask_in, mask_ref),
                (cnbr_in, cnbr_ref),
                (cmask_in, cmask_ref),
                (edge_in.at[pl.ds(1, 3)], edge_ref.at[pl.ds(1, 3)]),
                (node_in.at[pl.ds(1, 3)], node_ref.at[pl.ds(1, 3)]),
            )
        )
    ]
    for c in loads:
        c.start()

    def copy(k, src, dst, peer):
        return pltpu.make_async_remote_copy(
            src_ref=src,
            dst_ref=dst,
            send_sem=send_sem.at[k],
            recv_sem=recv_sem.at[k],
            device_id=peer,
            device_id_type=MESH,
        )

    def rim_copies(base, src, dst):
        return [
            copy(base, src.at[pl.ds(0, H)], dst.at[pl.ds(0, H)], (up, d)),
            copy(base + 1, src.at[pl.ds(H, H)], dst.at[pl.ds(H, H)], (down, d)),
            copy(base + 2, src.at[pl.ds(2 * H, 2 * H)], dst.at[pl.ds(2 * H, 2 * H)], (r, other)),
        ]

    def four_copies(base, low, high, dst):
        return [
            pltpu.make_async_remote_copy(
                src_ref=src,
                dst_ref=dst.at[2 * (1 - way) + cross],
                send_sem=send_sem.at[base + 2 * way + cross],
                recv_sem=recv_sem.at[base + 2 * (1 - way) + cross],
                device_id=(region, other if cross else d),
                device_id_type=MESH,
            )
            for way, src, region in ((0, low, down), (1, high, up))
            for cross in range(2)
        ]

    def four_arrivals(base, src, dst):
        return [copy(base + k, src, dst.at[k], (r, other)) for k in range(4)]

    tile_ref[...] = jnp.zeros_like(tile_ref)
    loads[0].wait()
    tile_ref[0:4, 0:H] = send_ref[...].astype(F32)
    lists = tile_ref[...].T
    lane = lax.broadcasted_iota(jnp.int32, (H, F), 1)
    picks = []
    for j in range(4):
        column = lists[0:H, j : j + 1].astype(jnp.int32)
        picks.append((lane == column).astype(F32).astype(BF16))
    pick_all[2 * SIDE :, :] = jnp.concatenate(picks, axis=0)

    loads[1].wait()
    x = x_ref[...]
    x_hi, x_lo = halves(x)
    rim_send[...] = dot(pick_all[2 * SIDE :, :], x_hi) + dot(pick_all[2 * SIDE :, :], x_lo)

    loads[2].wait()
    loads[3].wait()
    parent = parent_ref[...].reshape(1, F)
    share = share_ref[...].reshape(1, F).astype(F32)
    p_region = lax.shift_right_logical(parent, 8)
    p_local = parent & 255
    at_low = p_region == down
    at_high = p_region == up
    here = p_region == r
    own_hot[...] = one_hot(jnp.where(here, (p_local + C * d) & 255, -1), 2 * C)
    flags = jnp.concatenate(
        [at_low.astype(F32), at_high.astype(F32), jnp.zeros((14, F), F32)], axis=0
    ).astype(BF16)
    before = lax.broadcasted_iota(jnp.int32, (F, F), 0) <= lax.broadcasted_iota(
        jnp.int32, (F, F), 1
    )
    ranks = dot(flags, before.astype(F32).astype(BF16)).astype(jnp.int32) - 1
    low_rank = jnp.where(at_low, ranks[0:1], -1)
    high_rank = jnp.where(at_high, ranks[1:2], -1)
    pick_all[0 : 2 * SIDE, :] = jnp.concatenate(
        [one_hot(low_rank, SIDE), one_hot(high_rank, SIDE)], axis=0
    )
    side_pick = pick_all.at[pl.ds(0, 2 * SIDE)]
    rim_pick = pick_all.at[pl.ds(2 * SIDE, 4 * H)]
    number = jnp.where(at_high, high_rank + SIDE, low_rank) + 1
    src_proj[2 * W :, 0:F] = jnp.broadcast_to(number.astype(F32), (16, F)).astype(BF16)
    where_at = at_low.astype(F32) + 2.0 * at_high.astype(F32)
    facts = jnp.concatenate(
        [p_local.astype(F32), share, where_at, jnp.zeros((13, F), F32)], axis=0
    ).astype(BF16)
    meta_send[...] = dot_nt(facts, pick_all[...])[0:8]
    metas = four_copies(3, meta_send, meta_send, meta_recv)
    metas.append(copy(7, meta_send, meta_recv.at[4], (r, other)))
    shares16 = jnp.broadcast_to(share, (16, F)).astype(BF16)
    own_total = dot_nt(shares16, own_hot[...])[0:8]
    tot_send[:, 0:C] = own_total[:, C:]
    tot_send[:, C:] = own_total[:, 0:C]
    tot_copy = copy(8, tot_send, tot_recv, (r, other))

    pl.semaphore_wait(barrier, 7)
    rims = rim_copies(0, rim_send, rim_recv)
    for c in rims + metas + [tot_copy]:
        c.start()

    for c in loads[4:9]:
        c.wait()
    tile_ref[0:16, :] = bias_ref[...].reshape(16, W)
    biases = tile_ref[...].T

    def bias(layer, k, centre=False):
        column = biases[:, 4 * layer + k : 4 * layer + k + 1]
        return centred_bias(column) if centre else column

    def prepare(layer):
        for k in range(3):
            wts[6 * layer + k] = stacked(edge_ref[layer, k], centred=k == 2)
            wts[6 * layer + 3 + k] = stacked(node_ref[layer, k], centred=k == 2)

    side_twice = jnp.concatenate([side_pick[...], side_pick[...]], axis=0)

    def fine_own(layer, rows_split):
        own_ref[...] = fold(dot(wts[6 * layer], rows_split)) + bias(layer, 0)
        node_own[...] = fold(dot(wts[6 * layer + 3], rows_split)) + bias(layer, 2)
        src_proj[0 : 2 * W, 0:F] = split(fold(dot(wts[6 * layer + 1], rows_split)))

        def slot(s, carry):
            hot = one_hot(nbr_ref[pl.ds(s, 1), :], F)
            if layer == 0:
                gathered = dot(src_proj[:, 0:F], hot)
                side_ids[pl.ds(s, 1), :] = gathered[2 * W : 2 * W + 1].astype(jnp.int32) - 1
            else:
                gathered = dot(src_proj[0 : 2 * W, 0:F], hot)
            base_ref[s] = fold(gathered[0 : 2 * W]) + own_ref[...]
            return carry

        lax.fori_loop(0, SLOTS, slot, 0, unroll=4)

    def fine_rims(layer, rim_arrivals, rim_rows):
        for c in rim_arrivals:
            c.wait_recv()
        rim = jnp.concatenate(halves(rim_rows[...]), axis=1)
        src_proj[0 : 2 * W, F:] = split(fold(dot_nt(wts[6 * layer + 1], rim)))

    def fine_messages(layer, rows, extra_proj, extra_hot):
        total_ref[...] = jnp.zeros_like(total_ref)
        bias1 = jnp.broadcast_to(bias(layer, 1, True), (W, F))

        def slots(g, carry):
            members = [16 * g + k for k in range(16)]
            for t in range(0, F, 512):
                cols = pl.ds(t, 512)
                total = total_ref[:, cols]
                hidden = [
                    base_ref[s, :, cols] + fold(dot(extra_proj, extra_hot(s, cols)))
                    for s in members
                ]
                hidden = [split(jnp.maximum(h, 0.0)) for h in hidden]
                centred = [fold(dot(wts[6 * layer + 2], h)) + bias1[:, 0:512] for h in hidden]
                scales = [
                    scale_of(c) * mask_ref[pl.ds(s, 1), cols].astype(F32)
                    for c, s in zip(centred, members)
                ]
                for c, scale in zip(centred, scales):
                    total = total + c * scale
                total_ref[:, cols] = total
            return carry

        lax.fori_loop(0, SLOTS // 16, slots, 0, unroll=1)
        return node_update(
            rows,
            node_own[...],
            total_ref[...],
            wts[6 * layer + 4],
            wts[6 * layer + 5],
            bias(layer, 3, True),
        )

    def picked(values):
        return fold(dot_nt(split(values), side_twice))

    def paired(table):
        parts = jnp.concatenate([table & -16, table & 15], axis=0).astype(F32).astype(BF16)
        both = dot_nt(parts, side_twice)
        values = (both[0:SLOTS] + both[SLOTS:]).astype(jnp.int32)
        first = lax.broadcasted_iota(jnp.int32, (8, W), 1) < 2 * SIDE
        return jnp.where(first, values[0:8], values[8:16])

    def side_nodes(layer, rows):
        ids8 = paired(nbr_ref[...])
        valid8 = paired(mask_ref[...]).astype(F32)
        own4 = jnp.concatenate([picked(own_ref[...])] * 4, axis=1)
        bias1 = jnp.broadcast_to(bias(layer, 1, True), (W, 4 * W))
        total = jnp.zeros((W, 4 * W), F32)
        for g in range(2):
            ids = jnp.concatenate([ids8[4 * g + k : 4 * g + k + 1] for k in range(4)], axis=1)
            valid = jnp.concatenate([valid8[4 * g + k : 4 * g + k + 1] for k in range(4)], axis=1)
            hidden = fold(dot(src_proj[0 : 2 * W, :], one_hot(ids, F + 4 * H))) + own4
            total += message(hidden, wts[6 * layer + 2], bias1, valid)
        total = (total[:, 0:W] + total[:, W : 2 * W]) + (
            total[:, 2 * W : 3 * W] + total[:, 3 * W :]
        )
        total = total + pltpu.roll(total, 2 * SIDE, 1)
        return node_update(
            picked(rows),
            picked(node_own[...]),
            total,
            wts[6 * layer + 4],
            wts[6 * layer + 5],
            bias(layer, 3, True),
        )

    def coarse_layer(layer, rows, own_split, sources):
        own = fold(dot(wts[6 * layer], own_split)) + bias(layer, 0)
        node_part = fold(dot(wts[6 * layer + 3], own_split)) + bias(layer, 2)
        proj = split(fold(dot(wts[6 * layer + 1], sources())))
        own4 = jnp.concatenate([own] * 4, axis=1)
        bias1 = jnp.broadcast_to(bias(layer, 1, True), (W, 4 * C))
        id_rows, valid_rows = [], []
        for g in range(4):
            k = range(4 * g, 4 * g + 4)
            id_rows.append(jnp.concatenate([cnbr_ref[i : i + 1, :] for i in k], axis=1))
            valid_rows.append(
                jnp.concatenate([cmask_ref[i : i + 1, :] for i in k], axis=1).astype(F32)
            )
        hots = [one_hot((ids + C * d) & 255, 2 * C) for ids in id_rows]
        hidden = [split(jnp.maximum(fold(dot(proj, hot)) + own4, 0.0)) for hot in hots]
        centred = [fold(dot(wts[6 * layer + 2], h)) + bias1 for h in hidden]
        scales = [scale_of(c) * valid for c, valid in zip(centred, valid_rows)]
        total = centred[0] * scales[0] + centred[1] * scales[1]
        total = total + (centred[2] * scales[2] + centred[3] * scales[3])
        total = (total[:, 0:C] + total[:, C : 2 * C]) + (
            total[:, 2 * C : 3 * C] + total[:, 3 * C :]
        )
        return node_update(
            rows,
            node_part,
            total,
            wts[6 * layer + 4],
            wts[6 * layer + 5],
            bias(layer, 3, True),
        )

    prepare(0)
    rows = x.T
    fine_own(0, split(rows))
    for c in loads[9:]:
        c.wait()
    prepare(1)
    fine_rims(0, rims, rim_recv)

    side_share = dot_nt(shares16, side_twice)[0:1]
    side_send[...] = (side_nodes(0, rows) * side_share).T[0 : 2 * SIDE]
    low_rows = side_send.at[pl.ds(0, SIDE)]
    high_rows = side_send.at[pl.ds(SIDE, SIDE)]
    sides = four_copies(9, low_rows, high_rows, side_recv)
    for c in sides:
        c.start()
    def rim_hot(s, cols):
        return one_hot(nbr_ref[pl.ds(s, 1), cols] - F, 4 * H)

    fine_ref[...] = fine_messages(0, rows, src_proj[0 : 2 * W, F:], rim_hot)

    weighted = split(fine_ref[...] * share)
    partial = fold(dot_nt(weighted, own_hot[...]))
    part_send[:, 0:C] = partial[:, C:]
    part_send[:, C:] = partial[:, 0:C]
    part_copy = copy(13, part_send, part_recv, (r, other))
    part_copy.start()

    rim2_send[...] = fold_lanes(dot_nt(rim_pick[...], split(fine_ref[...])))
    rims2 = rim_copies(20, rim2_send, rim2_recv)
    for c in rims2:
        c.start()

    prepare(2)

    for c in four_arrivals(3, meta_send, meta_recv) + metas[4:]:
        c.wait_recv()
    tile_ref[0:40, :] = meta_recv[...].reshape(40, W)
    tile_ref[40:48, :] = meta_send[...]
    lists = tile_ref[...].T

    def listed(k, start, size, only=None):
        rows_at = slice(start, start + size)
        weight = lists[rows_at, 8 * k + 1 : 8 * k + 2]
        if only is not None:
            weight = jnp.where(lists[rows_at, 8 * k + 2 : 8 * k + 3] == only, weight, 0.0)
        return lists[rows_at, 8 * k : 8 * k + 1], weight

    def chosen(entries):
        wanted = jnp.concatenate([e[0] for e in entries], axis=0).astype(jnp.int32)
        weight = jnp.concatenate([e[1] for e in entries], axis=0)
        nodes = lax.broadcasted_iota(jnp.int32, (wanted.shape[0], 2 * C), 1)
        return nodes == ((wanted + C * d) & 255), weight

    match, weight_in = chosen(
        [listed(0, 32, 32), listed(1, 32, 32), listed(2, 0, 32), listed(3, 0, 32)]
    )
    side_hot = match.astype(F32).astype(BF16)
    side_total = jnp.sum(jnp.where(match, weight_in, 0.0), axis=0, keepdims=True)
    match, weight_out = chosen(
        [listed(2, 0, 32), listed(3, 96, 32, 1.0), listed(5, 64, 16, 0.0)]
        + [listed(0, 32, 32), listed(1, 96, 32, 2.0), listed(5, 80, 16, 0.0)]
        + [listed(2, 64, 16, 1.0), listed(0, 80, 16, 2.0)]
        + [listed(0, 64, 16, 2.0), listed(2, 80, 16, 1.0), listed(4, 96, 32, 0.0)]
    )
    out_hot = jnp.where(match, weight_out * 0.25, 0.0).astype(BF16)
    tot_copy.wait_recv()
    totals = own_total[0:1] + tot_recv[0:1, :] + side_total
    inverse = 1.0 / jnp.maximum(totals, 1.0)

    for c in four_arrivals(9, low_rows, side_recv):
        c.wait_recv()
    from_sides = fold(dot(split(side_recv[...].reshape(4 * SIDE, W).T), side_hot))
    part_copy.wait_recv()
    coarse = (partial + part_recv[...] + from_sides) * inverse

    group = split(coarse)
    mid = coarse_layer(1, coarse[:, 0:C], group[:, 0:C], lambda: group)
    mid_send[...] = mid
    mid_copy = copy(14, mid_send, mid_recv, (r, other))
    mid_copy.start()
    mid_split = split(mid)
    prepare(3)

    def mid_sources():
        mid_copy.wait_recv()
        return jnp.concatenate([mid_split, split(mid_recv[...])], axis=1)

    coarse_out = coarse_layer(2, mid, mid_split, mid_sources)
    co_split = split(coarse_out)
    co_send[...] = coarse_out
    co_copy = copy(15, co_send, co_recv, (r, other))
    co_copy.start()
    cout_ref[...] = coarse_out.T

    co_copy.wait_recv()
    known = jnp.concatenate([co_split, split(co_recv[...])], axis=1)
    given = fold_lanes(dot_nt(out_hot, known))
    pay_send[...] = given[0:192]
    pays = [
        copy(
            16 + k,
            pay_send.at[pl.ds(start, size)],
            pay_recv.at[pl.ds(start, size)],
            (region, d),
        )
        for k, (start, size, region) in enumerate(
            ((0, 80, up), (80, 80, down), (160, 16, up2), (176, 16, down2))
        )
    ]
    for c in pays:
        c.start()
    rows = fine_ref[...] + (share * 0.25) * fold(dot(known, own_hot[...]))
    fine_own(3, split(rows))

    for c in rims2 + pays:
        c.wait_recv()
    from_low, from_high = pay_recv[0:32, :], pay_recv[80:112, :]
    rim = rim2_recv[...] + given[192:256]
    rim += jnp.concatenate(
        [
            pay_recv[64:80, :] + pay_recv[160:176, :],
            pay_recv[144:160, :] + pay_recv[176:192, :],
            pay_recv[32:64, :] + pay_recv[112:144, :],
        ],
        axis=0,
    )
    late = jnp.concatenate([rim, from_low, from_high], axis=0)
    late_split = split(late.T)
    side_split = late_split[:, 4 * H :]
    extra = jnp.concatenate(
        [split(fold(dot(wts[19], late_split))), split(fold(dot(wts[18], side_split)))], axis=1
    )
    rows += fold(dot(side_split, side_pick[...]))
    node_own[...] += fold(dot(split(fold(dot(wts[21], side_split))), side_pick[...]))

    def late_hot(s, cols):
        return jnp.concatenate(
            [
                one_hot(nbr_ref[pl.ds(s, 1), cols] - F, 4 * H),
                one_hot(side_ids[pl.ds(s, 1), cols], 2 * SIDE),
                side_pick[:, cols],
            ],
            axis=0,
        )

    out_ref[...] = fine_messages(3, rows, extra, late_hot).T

    sent = rims + metas + [tot_copy] + sides + [part_copy, mid_copy, co_copy] + pays + rims2
    for c in sent:
        c.wait_send()


def hand_over(fine_in, coarse_in, fine_out, coarse_out, fine_tile, coarse_tile, sems):
    size = F // 4
    pieces = [(fine_in.at[pl.ds(k * size, size)], fine_tile.at[k], fine_out.at[pl.ds(k * size, size)]) for k in range(4)]
    pieces.append((coarse_in, coarse_tile, coarse_out))
    taken = [pltpu.make_async_copy(a, b, sems.at[k]) for k, (a, b, _) in enumerate(pieces)]
    given = [pltpu.make_async_copy(b, c, sems.at[5 + k]) for k, (_, b, c) in enumerate(pieces)]
    for c in taken:
        c.start()
    for t, g in zip(taken, given):
        t.wait()
        g.start()
    for g in given:
        g.wait()


def body(regions, *args):
    vmem = pl.BlockSpec(memory_space=pltpu.VMEM)
    results = (
        jax.ShapeDtypeStruct((F, W), F32),
        jax.ShapeDtypeStruct((C, W), F32),
    )
    whole = pl.BlockSpec(memory_space=pl.ANY)
    fine, coarse = pl.pallas_call(
        functools.partial(kernel, regions),
        out_shape=results,
        in_specs=[whole] * 11,
        out_specs=(vmem, vmem),
        scratch_shapes=[pltpu.VMEM(a.shape, a.dtype) for a in args]
        + [
            pltpu.VMEM((W, W), F32),
            pltpu.VMEM((24, 2 * W, 2 * W), BF16),
            pltpu.VMEM((SLOTS, W, F), F32),
            pltpu.VMEM((2 * W + 16, F + 4 * H), BF16),
            pltpu.VMEM((W, F), F32),
            pltpu.VMEM((W, F), F32),
            pltpu.VMEM((W, F), F32),
            pltpu.VMEM((W, F), F32),
            pltpu.VMEM((2 * SIDE + 4 * H, F), BF16),
            pltpu.VMEM((2 * C, F), BF16),
            pltpu.VMEM((SLOTS, F), jnp.int32),
            pltpu.VMEM((4 * H, W), F32),
            pltpu.VMEM((4 * H, W), F32),
            pltpu.VMEM((8, W), F32),
            pltpu.VMEM((5, 8, W), F32),
            pltpu.VMEM((8, 2 * C), F32),
            pltpu.VMEM((8, 2 * C), F32),
            pltpu.VMEM((W, 2 * C), F32),
            pltpu.VMEM((W, 2 * C), F32),
            pltpu.VMEM((2 * SIDE, W), F32),
            pltpu.VMEM((4, SIDE, W), F32),
            pltpu.VMEM((W, C), F32),
            pltpu.VMEM((W, C), F32),
            pltpu.VMEM((W, C), F32),
            pltpu.VMEM((W, C), F32),
            pltpu.VMEM((192, W), F32),
            pltpu.VMEM((192, W), F32),
            pltpu.VMEM((4 * H, W), F32),
            pltpu.VMEM((4 * H, W), F32),
            pltpu.SemaphoreType.DMA((23,)),
            pltpu.SemaphoreType.DMA((23,)),
            pltpu.SemaphoreType.DMA((13,)),
        ],
        compiler_params=pltpu.CompilerParams(collective_id=0, has_side_effects=True),
    )(*args)
    return pl.pallas_call(
        hand_over,
        out_shape=results,
        in_specs=[whole] * 2,
        out_specs=(whole, whole),
        scratch_shapes=[
            pltpu.VMEM((4, F // 4, W), F32),
            pltpu.VMEM((C, W), F32),
            pltpu.SemaphoreType.DMA((10,)),
        ],
    )(fine, coarse)


def solution(mesh):
    both = ("region", "dom")
    return jax.shard_map(
        functools.partial(body, mesh.shape["region"]),
        mesh=mesh,
        in_specs=(
            P(both, None),
            P(None, both),
            P(None, both),
            P(None, both),
            P(None, both),
            P(None, both),
            P(both),
            P(both),
            P(),
            P(),
            P(),
        ),
        out_specs=(P(both, None), P(both, None)),
        check_vma=False,
    )
```
